256 devices in a mesh: mem: 16 (over z, core), reg: 16 (over x, y).
Axes of the slice: x: 4, y: 4, z: 8, core: 2. Of those that a mesh axis runs over, the one named last changes fastest.
Arguments:
- member_vectors: float32 [131072, 2048], P('reg', 'mem'), may hold values from -6 to 6
- flow_speed_ratio: float32 [131072], P('reg'), may hold values from 0.3 to 0.95
- obs_pert: bfloat16 [8192, 2048], P('reg', 'mem'), may hold values from -6 to 6
- obs_incr: bfloat16 [8192, 2048], P('reg', 'mem'), may hold values from -12 to 12
- edge_list: int32 [16, 2, 64], P('reg'), may hold values from 0 to 511
- block_obs: int32 [2048, 64], P('reg'), may hold values from 0 to 639
- block_count: int32 [2048], P('reg'), may hold values from 1 to 64
- obs_offset: float32 [2048, 64], P('reg'), may hold values from -64 to 128
Outputs:
- analysis: float32 [131072, 2048], P('reg', 'mem')
The draws below stay inside these ranges and needn't reach their ends.
All inputs are finite; a program needn't handle non-finite values.
Results may differ from the reference program's by a relative error of at most 0.0014.
Values may be sent and summed in bfloat16 or wider, within the bound.
A program may use at most 128 MiB of HBM per device.

```python
import jax
import jax.numpy as jnp
from jax import lax

DOMAIN_POINTS = 8192
OBS_REG = 512
BLOCK = 64
KB = 64
EDGE = 64
STEPS = 4
MEMBERS = 2048
REGIONS = 16
CELLS = 131072
OBS = 8192
NB_REG = 128
NBLOCKS = 2048
OBS_EXT = 640
N_REG = 16


def set_ends(values, key, low, high):
    longest = values.shape.index(max(values.shape))
    spots = []
    for shift in (0, 1):
        where = [jax.random.randint(jax.random.fold_in(key, axis), (), 0, length) for axis, length in enumerate(values.shape)]
        where[longest] = (where[longest] + shift) % values.shape[longest]
        spots.append(tuple(where))
    return values.at[spots[0]].set(low).at[spots[1]].set(high)


def block_scale(stream_key, extent, shards, smallest, high):
    def one(dim, shards_of):
        steps = jax.random.uniform(jax.random.fold_in(jax.random.fold_in(stream_key, 6), dim), (shards_of,), jnp.float32, smallest / len(shards), high / len(shards))
        return jnp.repeat(jnp.exp(steps), extent[dim] // shards_of).reshape((-1,) + (1,) * (len(extent) - dim - 1))

    level = one(*shards[0])
    for cut in shards[1:]:
        level = level * one(*cut)
    return level


def scatter_about(key, extent, width, limit, shards=(), kind=jnp.bfloat16):
    entries = width * jax.random.normal(key, extent, jnp.float32)
    if shards:
        entries = entries * block_scale(key, extent, shards, -0.22, 0.18)
    return jnp.clip(entries, -limit, limit).astype(kind)


def setup_inputs(seed: int = 0) -> dict:
    key_list = jax.random.split(jax.random.key(seed), 9)
    return {
        "member_vectors": scatter_about(key_list[0], (CELLS, MEMBERS), 1.0, 6.0, ((0, 16), (1, 16)), jnp.float32),
        "flow_speed_ratio": jnp.clip(0.3 + 0.65 * jax.random.uniform(key_list[1], (CELLS,), jnp.float32) ** block_scale(key_list[1], (CELLS,), ((0, 16),), -0.2, 0.2), 0.3, 0.95),
        "obs_pert": scatter_about(key_list[2], (OBS, MEMBERS), 1.0, 6.0, ((0, 16), (1, 16))),
        "obs_incr": scatter_about(key_list[3], (OBS, MEMBERS), 2.0, 12.0, ((0, 16), (1, 16))),
        "edge_list": set_ends(jax.random.randint(key_list[4], (REGIONS, 2, EDGE), 0, OBS_REG), jax.random.fold_in(key_list[4], 1), 0, OBS_REG - 1).astype(jnp.int32),
        "block_obs": set_ends(jax.random.randint(key_list[5], (NBLOCKS, KB), 0, OBS_EXT), jax.random.fold_in(key_list[5], 1), 0, OBS_EXT - 1).astype(jnp.int32),
        "block_count": set_ends(jax.random.randint(key_list[6], (NBLOCKS,), 1, KB + 1), jax.random.fold_in(key_list[6], 1), 1, KB).astype(jnp.int32),
        "obs_offset": jnp.clip(-64.0 + 192.0 * jax.random.uniform(key_list[7], (NBLOCKS, KB), jnp.float32) ** block_scale(key_list[7], (NBLOCKS, KB), ((0, 16),), -0.2, 0.2), -64.0, 128.0),
    }


def donor_scheme_advect(member_vectors, flow_speed_ratio):
    concentration_map = member_vectors
    for sweep in range(STEPS):
        concentration_map = concentration_map - flow_speed_ratio[:, None] * (concentration_map - jnp.roll(concentration_map, 1, axis=0))
    return concentration_map


def taper_mask(positions, live_counts):
    position = jnp.arange(BLOCK).astype(jnp.float32)
    distance = (position[None, :, None] - positions[:, None, :]) / (0.5 * BLOCK)
    active = jnp.arange(KB).astype(jnp.int32)[None, :] < live_counts[:, None]
    return jnp.where(active[:, None, :], 1.0 / (1.0 + distance * distance), 0.0)


def reference(member_vectors, flow_speed_ratio, obs_pert, obs_incr, edge_list, block_obs, block_count, obs_offset):
    predicted_estimate = donor_scheme_advect(member_vectors, flow_speed_ratio)
    first_guess_state = predicted_estimate.astype(jnp.bfloat16)

    def region_table(table, nearby_domain):
        lower = (nearby_domain - 1 + N_REG) % N_REG
        upper = (nearby_domain + 1) % N_REG
        own = lax.dynamic_slice_in_dim(table, (nearby_domain * OBS_REG).astype(jnp.int32), OBS_REG, 0)
        lower_rows = lax.dynamic_slice_in_dim(table, (lower * OBS_REG).astype(jnp.int32), OBS_REG, 0)
        upper_rows = lax.dynamic_slice_in_dim(table, (upper * OBS_REG).astype(jnp.int32), OBS_REG, 0)
        return jnp.concatenate([lower_rows[edge_list[lower, 1]], own, upper_rows[edge_list[upper, 0]]], 0)

    def region_increment(nearby_domain):
        ext_p = region_table(obs_pert, nearby_domain)
        ext_i = region_table(obs_incr, nearby_domain)
        first = (nearby_domain * NB_REG).astype(jnp.int32)
        obs_lists = lax.dynamic_slice_in_dim(block_obs, first, NB_REG, 0)
        live_counts = lax.dynamic_slice_in_dim(block_count, first, NB_REG, 0)
        positions = lax.dynamic_slice_in_dim(obs_offset, first, NB_REG, 0)
        mesh_point_entries = lax.dynamic_slice_in_dim(first_guess_state, (nearby_domain * DOMAIN_POINTS).astype(jnp.int32), DOMAIN_POINTS, 0)
        mesh_point_entries = mesh_point_entries.reshape(NB_REG, BLOCK, MEMBERS).astype(jnp.float32)
        obs_rows = ext_p[obs_lists].astype(jnp.float32)
        incr_rows = ext_i[obs_lists].astype(jnp.float32)
        cross = jnp.einsum('bcm,bkm->bck', mesh_point_entries, obs_rows)
        sum_cells = jnp.sum(mesh_point_entries, 2)
        sum_obs = jnp.sum(obs_rows, 2)
        covariance = ((cross - sum_cells[:, :, None] * sum_obs[:, None, :] / MEMBERS) / (MEMBERS - 1)
                      * taper_mask(positions, live_counts)).astype(jnp.bfloat16)
        correction_delta = jnp.einsum('bck,bkm->bcm', covariance.astype(jnp.float32), incr_rows)
        return correction_delta.astype(jnp.bfloat16).reshape(DOMAIN_POINTS, MEMBERS)

    regions_all = jnp.arange(N_REG).astype(jnp.int32)
    stacked = lax.map(region_increment, regions_all)
    correction_delta = stacked.reshape(CELLS, MEMBERS)
    return predicted_estimate + correction_delta.astype(jnp.float32)
```

```python
import jax
import jax.numpy as jnp
from jax import lax
from jax.sharding import PartitionSpec as P

BLOCK = 64
KB = 64
STEPS = 4


def passed_along(block, axis, distance):
    devices = range(lax.axis_size(axis))
    route = [((i - distance) % len(devices), i) for i in devices]
    return lax.ppermute(block, axis, route)


def padded(block, sides, width):
    for axis, dim in sides:
        count = lax.axis_size(axis)
        forward = [(i, i + 1) for i in range(count - 1)]
        forward.append((count - 1, 0))
        backward = [(target, source) for source, target in forward]
        low = lax.ppermute(
            lax.slice_in_dim(block, block.shape[dim] - width, None, axis=dim), axis, forward
        )
        high = lax.ppermute(lax.slice_in_dim(block, 0, width, axis=dim), axis, backward)
        block = jnp.concatenate([low, block, high], axis=dim)
    return block


def side_by_side(arrays, axis, dim, along):
    columns = [a.reshape(*a.shape[:along], -1) for a in arrays]
    both = jnp.concatenate(columns, axis=along)
    whole, at, gathered = (lax.psum_scatter(both, axis, scatter_dimension=dim, tiled=True), 0, [])
    for a, column in zip(arrays, columns):
        piece = whole[..., at : at + column.shape[along]]
        gathered.append(piece.reshape(*piece.shape[:along], *a.shape[along:]))
        at += column.shape[along]
    return tuple(gathered)


def laid_out(parts, dim):
    parts = jnp.moveaxis(parts, 0, dim)
    lengths = parts.shape
    return parts.reshape(*lengths[:dim], lengths[dim] * lengths[dim + 1], *lengths[dim + 2 :])


def from_everyone(value, axis):
    copies = jnp.broadcast_to(value, (lax.axis_size(axis), *value.shape))
    return lax.all_to_all(copies, axis, split_axis=0, concat_axis=0, tiled=True)


def gathered_copies(value, axis, dim):
    return laid_out(from_everyone(value, axis), dim)


def taper_mask(positions, live_counts):
    position = jnp.arange(BLOCK).astype(jnp.float32)
    distance = (position[None, :, None] - positions[:, None, :]) / (0.5 * BLOCK)
    active = jnp.arange(KB)[None, :] < live_counts[:, None]
    return jnp.where(active[:, None, :], 1.0 / (1.0 + distance * distance), 0.0)


def block_sums(mesh_point_entries, obs_rows):
    cross = jnp.einsum(
        "bcm,bkm->bck", mesh_point_entries, obs_rows, preferred_element_type=jnp.float32
    )
    sum_cells = jnp.sum(mesh_point_entries.astype(jnp.float32), 2)
    sum_obs = jnp.sum(obs_rows.astype(jnp.float32), 2)
    return (cross, sum_cells, sum_obs)


def covariances(cross, sum_cells, sum_obs, positions, live_counts, members):
    return (
        (cross - sum_cells[:, :, None] * sum_obs[:, None, :] / members)
        / (members - 1)
        * taper_mask(positions, live_counts)
    ).astype(jnp.bfloat16)


def apply_cov(covariance, incr_rows):
    correction_delta = jnp.einsum(
        "bck,bkm->bcm", covariance, incr_rows, preferred_element_type=jnp.float32
    )
    return correction_delta.astype(jnp.bfloat16)


def per_device(
    member_vectors,
    flow_speed_ratio,
    obs_pert,
    obs_incr,
    edge_list,
    block_obs,
    block_count,
    obs_offset,
):
    concentration_map = member_vectors
    outgoing = jnp.concatenate([concentration_map[-STEPS:, :], flow_speed_ratio[-STEPS:, None]], 1)
    arrived = passed_along(outgoing, "reg", 1)
    widened = jnp.concatenate([arrived[:, :-1], concentration_map], 0)
    speeds = jnp.concatenate([arrived[:, -1], flow_speed_ratio], 0)
    for sweep in range(STEPS):
        widened = widened[1:] - speeds[sweep + 1 :, None] * (widened[1:] - widened[:-1])
    concentration_map = widened
    first_guess_state = concentration_map.astype(jnp.bfloat16)
    lend = edge_list.shape[2]
    edge_rows = edge_list.reshape(-1)
    chosen = jnp.stack([obs_pert[edge_rows], obs_incr[edge_rows]])
    rimmed = padded(chosen, (("reg", 1),), lend)
    extended = jnp.concatenate(
        [rimmed[:, :lend], jnp.stack([obs_pert, obs_incr]), rimmed[:, -lend:]], 1
    )
    member_dev = member_vectors.shape[1]
    members = member_dev * lax.axis_size("mem")
    per_region = block_obs.shape[0]
    share = per_region // lax.axis_size("mem")
    mesh_point_entries = first_guess_state.reshape(per_region, BLOCK, member_dev)
    slots = extended.shape[1]
    picks = (block_obs.reshape(-1)[:, None] == jnp.arange(slots)[None, :]).astype(jnp.bfloat16)
    both = jnp.concatenate([extended[0], extended[1]], 1)
    rows = jnp.dot(picks, both, preferred_element_type=jnp.float32).astype(jnp.bfloat16)
    obs_rows = rows[:, :member_dev].reshape(per_region, KB, member_dev)
    incr_rows = rows[:, member_dev:].reshape(per_region, KB, member_dev)
    partial_value = block_sums(mesh_point_entries, obs_rows)
    cross, sum_cells, sum_obs = side_by_side(
        (partial_value[0], partial_value[1], partial_value[2]), "mem", 0, 2
    )
    first_block = lax.axis_index("mem") * share
    live_counts = lax.dynamic_slice_in_dim(block_count, first_block, share, 0)
    positions = lax.dynamic_slice_in_dim(obs_offset, first_block, share, 0)
    own_cov = covariances(cross, sum_cells, sum_obs, positions, live_counts, members)
    covariance = gathered_copies(own_cov, "mem", 0)
    correction_delta = apply_cov(covariance, incr_rows)
    returned = correction_delta.reshape(per_region * BLOCK, member_dev)
    return concentration_map + returned.astype(jnp.float32)


def solution(mesh):
    return jax.shard_map(
        per_device,
        mesh=mesh,
        in_specs=(
            P("reg", "mem"),
            P("reg"),
            P("reg", "mem"),
            P("reg", "mem"),
            P("reg", None, None),
            P("reg", None),
            P("reg"),
            P("reg", None),
        ),
        out_specs=P("reg", "mem"),
        check_vma=False,
    )
```

```python
import jax
import jax.numpy as jnp
from jax import lax
from jax.sharding import PartitionSpec as P

BLOCK = 64
KB = 64
STEPS = 4


def passed_along(block, axis, distance):
    devices = range(lax.axis_size(axis))
    route = [((i - distance) % len(devices), i) for i in devices]
    return lax.ppermute(block, axis, route)


def padded(block, sides, width):
    for axis, dim in sides:
        count = lax.axis_size(axis)
        forward = [(i, i + 1) for i in range(count - 1)]
        forward.append((count - 1, 0))
        backward = [(target, source) for source, target in forward]
        low = lax.ppermute(
            lax.slice_in_dim(block, block.shape[dim] - width, None, axis=dim), axis, forward
        )
        high = lax.ppermute(lax.slice_in_dim(block, 0, width, axis=dim), axis, backward)
        block = jnp.concatenate([low, block, high], axis=dim)
    return block


def side_by_side(arrays, axis, dim, along):
    columns = [a.reshape(*a.shape[:along], -1) for a in arrays]
    both = jnp.concatenate(columns, axis=along)
    whole, at, gathered = (lax.psum_scatter(both, axis, scatter_dimension=dim, tiled=True), 0, [])
    for a, column in zip(arrays, columns):
        piece = whole[..., at : at + column.shape[along]]
        gathered.append(piece.reshape(*piece.shape[:along], *a.shape[along:]))
        at += column.shape[along]
    return tuple(gathered)


def laid_out(parts, dim):
    parts = jnp.moveaxis(parts, 0, dim)
    lengths = parts.shape
    return parts.reshape(*lengths[:dim], lengths[dim] * lengths[dim + 1], *lengths[dim + 2 :])


def from_everyone(value, axis):
    copies = jnp.broadcast_to(value, (lax.axis_size(axis), *value.shape))
    return lax.all_to_all(copies, axis, split_axis=0, concat_axis=0, tiled=True)


def gathered_copies(value, axis, dim):
    return laid_out(from_everyone(value, axis), dim)


def taper_mask(positions, live_counts):
    position = jnp.arange(BLOCK).astype(jnp.float32)
    distance = (position[None, :, None] - positions[:, None, :]) / (0.5 * BLOCK)
    active = jnp.arange(KB)[None, :] < live_counts[:, None]
    return jnp.where(active[:, None, :], 1.0 / (1.0 + distance * distance), 0.0)


def block_sums(mesh_point_entries, obs_rows):
    cross = jnp.einsum(
        "bcm,bkm->bck", mesh_point_entries, obs_rows, preferred_element_type=jnp.float32
    )
    sum_cells = jnp.sum(mesh_point_entries.astype(jnp.float32), 2)
    sum_obs = jnp.sum(obs_rows.astype(jnp.float32), 2)
    return (cross, sum_cells, sum_obs)


def covariances(cross, sum_cells, sum_obs, positions, live_counts, members):
    return (
        (cross - sum_cells[:, :, None] * sum_obs[:, None, :] / members)
        / (members - 1)
        * taper_mask(positions, live_counts)
    ).astype(jnp.bfloat16)


def apply_cov(covariance, incr_rows):
    correction_delta = jnp.einsum(
        "bck,bkm->bcm", covariance, incr_rows, preferred_element_type=jnp.float32
    )
    return correction_delta.astype(jnp.bfloat16)


def per_device(
    member_vectors,
    flow_speed_ratio,
    obs_pert,
    obs_incr,
    edge_list,
    block_obs,
    block_count,
    obs_offset,
):
    concentration_map = member_vectors
    outgoing = jnp.concatenate([concentration_map[-STEPS:, :], flow_speed_ratio[-STEPS:, None]], 1)
    arrived = passed_along(outgoing, "reg", 1)
    widened = jnp.concatenate([arrived[:, :-1], concentration_map], 0)
    speeds = jnp.concatenate([arrived[:, -1], flow_speed_ratio], 0)
    for sweep in range(STEPS):
        widened = widened[1:] - speeds[sweep + 1 :, None] * (widened[1:] - widened[:-1])
    concentration_map = widened
    first_guess_state = concentration_map.astype(jnp.bfloat16)
    lend = edge_list.shape[2]
    edge_rows = edge_list.reshape(-1)
    chosen = jnp.stack([obs_pert[edge_rows], obs_incr[edge_rows]])
    rimmed = padded(chosen, (("reg", 1),), lend)
    extended = jnp.concatenate(
        [rimmed[:, :lend], jnp.stack([obs_pert, obs_incr]), rimmed[:, -lend:]], 1
    )
    member_dev = member_vectors.shape[1]
    members = member_dev * lax.axis_size("mem")
    per_region = block_obs.shape[0]
    share = per_region // lax.axis_size("mem")
    mesh_point_entries = first_guess_state.reshape(per_region, BLOCK, member_dev)
    slots = extended.shape[1]
    picks = (block_obs.reshape(-1)[:, None] == jnp.arange(slots)[None, :]).astype(jnp.bfloat16)
    both = jnp.concatenate([extended[0], extended[1]], 1)
    rows = jnp.dot(picks, both, preferred_element_type=jnp.float32).astype(jnp.bfloat16)
    obs_rows = rows[:, :member_dev].reshape(per_region, KB, member_dev)
    incr_rows = rows[:, member_dev:].reshape(per_region, KB, member_dev)
    partial_value = block_sums(mesh_point_entries, obs_rows)
    flat = BLOCK * KB
    payload = jnp.concatenate(
        [partial_value[0].reshape(per_region, flat), partial_value[1], partial_value[2]], 1
    )
    parts = lax.axis_size("mem")
    got = lax.psum_scatter(payload.reshape(parts, share, -1), "mem", scatter_dimension=0, tiled=True)
    got = got.reshape(share, -1)
    cross = got[:, :flat].reshape(share, BLOCK, KB)
    sum_cells = got[:, flat : flat + BLOCK]
    sum_obs = got[:, flat + BLOCK :]
    first_block = lax.axis_index("mem") * share
    live_counts = lax.dynamic_slice_in_dim(block_count, first_block, share, 0)
    positions = lax.dynamic_slice_in_dim(obs_offset, first_block, share, 0)
    own_cov = covariances(cross, sum_cells, sum_obs, positions, live_counts, members)
    covariance = gathered_copies(own_cov, "mem", 0)
    correction_delta = apply_cov(covariance, incr_rows)
    returned = correction_delta.reshape(per_region * BLOCK, member_dev)
    return concentration_map + returned.astype(jnp.float32)


def solution(mesh):
    return jax.shard_map(
        per_device,
        mesh=mesh,
        in_specs=(
            P("reg", "mem"),
            P("reg"),
            P("reg", "mem"),
            P("reg", "mem"),
            P("reg", None, None),
            P("reg", None),
            P("reg"),
            P("reg", None),
        ),
        out_specs=P("reg", "mem"),
        check_vma=False,
    )
```

```python
import jax
import jax.numpy as jnp
from jax import lax
from jax.experimental import pallas as pl
from jax.experimental.pallas import tpu as pltpu
from jax.sharding import PartitionSpec as P

BLOCK = 64
KB = 64
STEPS = 4
ROWS = 1024

def advect_kernel(halo_ref, s_ref, x_ref, f_ref, fb_ref, carry_ref):
    @pl.when(pl.program_id(0) == 0)
    def _():
        carry_ref[...] = halo_ref[...]
    x = x_ref[...]
    s = jnp.broadcast_to(s_ref[...], x.shape)
    first = lax.broadcasted_iota(jnp.int32, x.shape, 0) == 0
    last = x.shape[0] - 1
    for k in range(STEPS):
        before = jnp.where(first, carry_ref[k : k + 1, :], pltpu.roll(x, 1, 0))
        carry_ref[k : k + 1, :] = x[last:, :]
        x = x - s * (x - before)
    f_ref[...] = x
    fb_ref[...] = x.astype(jnp.bfloat16)

def advect(halo, speeds, x, interpret=False):
    cells, width = x.shape
    rows = min(ROWS, cells)
    return pl.pallas_call(
        advect_kernel,
        grid=(cells // rows,),
        in_specs=[
            pl.BlockSpec((8, width), lambda t: (0, 0)),
            pl.BlockSpec((rows, 1), lambda t: (t, 0)),
            pl.BlockSpec((rows, width), lambda t: (t, 0)),
        ],
        out_specs=[pl.BlockSpec((rows, width), lambda t: (t, 0)), pl.BlockSpec((rows, width), lambda t: (t, 0))],
        out_shape=[jax.ShapeDtypeStruct(x.shape, jnp.float32), jax.ShapeDtypeStruct(x.shape, jnp.bfloat16)],
        scratch_shapes=[pltpu.VMEM((8, width), jnp.float32)],
        compiler_params=pltpu.CompilerParams(dimension_semantics=("arbitrary",)),
        interpret=interpret,
    )(halo, speeds[:, None], x)

def halo_rows(arrived, arrived_speeds, width):
    v = arrived
    rows = [v[-1]]
    for k in range(1, STEPS):
        v = v[1:] - arrived_speeds[k:, None] * (v[1:] - v[:-1])
        rows.append(v[-1])
    return jnp.concatenate([jnp.stack(rows), jnp.zeros((8 - STEPS, width), v.dtype)], 0)


def passed_along(block, axis, distance):
    devices = range(lax.axis_size(axis))
    route = [((i - distance) % len(devices), i) for i in devices]
    return lax.ppermute(block, axis, route)


def padded(block, sides, width):
    for axis, dim in sides:
        count = lax.axis_size(axis)
        forward = [(i, i + 1) for i in range(count - 1)]
        forward.append((count - 1, 0))
        backward = [(target, source) for source, target in forward]
        low = lax.ppermute(
            lax.slice_in_dim(block, block.shape[dim] - width, None, axis=dim), axis, forward
        )
        high = lax.ppermute(lax.slice_in_dim(block, 0, width, axis=dim), axis, backward)
        block = jnp.concatenate([low, block, high], axis=dim)
    return block


def side_by_side(arrays, axis, dim, along):
    columns = [a.reshape(*a.shape[:along], -1) for a in arrays]
    both = jnp.concatenate(columns, axis=along)
    whole, at, gathered = (lax.psum_scatter(both, axis, scatter_dimension=dim, tiled=True), 0, [])
    for a, column in zip(arrays, columns):
        piece = whole[..., at : at + column.shape[along]]
        gathered.append(piece.reshape(*piece.shape[:along], *a.shape[along:]))
        at += column.shape[along]
    return tuple(gathered)


def laid_out(parts, dim):
    parts = jnp.moveaxis(parts, 0, dim)
    lengths = parts.shape
    return parts.reshape(*lengths[:dim], lengths[dim] * lengths[dim + 1], *lengths[dim + 2 :])


def from_everyone(value, axis):
    copies = jnp.broadcast_to(value, (lax.axis_size(axis), *value.shape))
    return lax.all_to_all(copies, axis, split_axis=0, concat_axis=0, tiled=True)


def gathered_copies(value, axis, dim):
    return laid_out(from_everyone(value, axis), dim)


def taper_mask(positions, live_counts):
    position = jnp.arange(BLOCK).astype(jnp.float32)
    distance = (position[None, :, None] - positions[:, None, :]) / (0.5 * BLOCK)
    active = jnp.arange(KB)[None, :] < live_counts[:, None]
    return jnp.where(active[:, None, :], 1.0 / (1.0 + distance * distance), 0.0)


def block_sums(mesh_point_entries, obs_rows):
    cross = jnp.einsum(
        "bcm,bkm->bck", mesh_point_entries, obs_rows, preferred_element_type=jnp.float32
    )
    sum_cells = jnp.sum(mesh_point_entries.astype(jnp.float32), 2)
    sum_obs = jnp.sum(obs_rows.astype(jnp.float32), 2)
    return (cross, sum_cells, sum_obs)


def covariances(cross, sum_cells, sum_obs, positions, live_counts, members):
    return (
        (cross - sum_cells[:, :, None] * sum_obs[:, None, :] / members)
        / (members - 1)
        * taper_mask(positions, live_counts)
    ).astype(jnp.bfloat16)


def apply_cov(covariance, incr_rows):
    correction_delta = jnp.einsum(
        "bck,bkm->bcm", covariance, incr_rows, preferred_element_type=jnp.float32
    )
    return correction_delta.astype(jnp.bfloat16)


def per_device(
    member_vectors,
    flow_speed_ratio,
    obs_pert,
    obs_incr,
    edge_list,
    block_obs,
    block_count,
    obs_offset,
):
    concentration_map = member_vectors
    outgoing = jnp.concatenate([concentration_map[-STEPS:, :], flow_speed_ratio[-STEPS:, None]], 1)
    arrived = passed_along(outgoing, "reg", 1)
    width = concentration_map.shape[1]
    halo = halo_rows(arrived[:, :-1], arrived[:, -1], width)
    concentration_map, first_guess_state = advect(halo, flow_speed_ratio, concentration_map)
    lend = edge_list.shape[2]
    edge_rows = edge_list.reshape(-1)
    chosen = jnp.stack([obs_pert[edge_rows], obs_incr[edge_rows]])
    rimmed = padded(chosen, (("reg", 1),), lend)
    extended = jnp.concatenate(
        [rimmed[:, :lend], jnp.stack([obs_pert, obs_incr]), rimmed[:, -lend:]], 1
    )
    member_dev = member_vectors.shape[1]
    members = member_dev * lax.axis_size("mem")
    per_region = block_obs.shape[0]
    share = per_region // lax.axis_size("mem")
    mesh_point_entries = first_guess_state.reshape(per_region, BLOCK, member_dev)
    slots = extended.shape[1]
    picks = (block_obs.reshape(-1)[:, None] == jnp.arange(slots)[None, :]).astype(jnp.bfloat16)
    both = jnp.concatenate([extended[0], extended[1]], 1)
    rows = jnp.dot(picks, both, preferred_element_type=jnp.float32).astype(jnp.bfloat16)
    obs_rows = rows[:, :member_dev].reshape(per_region, KB, member_dev)
    incr_rows = rows[:, member_dev:].reshape(per_region, KB, member_dev)
    partial_value = block_sums(mesh_point_entries, obs_rows)
    flat = BLOCK * KB
    payload = jnp.concatenate(
        [partial_value[0].reshape(per_region, flat), partial_value[1], partial_value[2]], 1
    )
    parts = lax.axis_size("mem")
    got = lax.psum_scatter(payload.reshape(parts, share, -1), "mem", scatter_dimension=0, tiled=True)
    got = got.reshape(share, -1)
    cross = got[:, :flat].reshape(share, BLOCK, KB)
    sum_cells = got[:, flat : flat + BLOCK]
    sum_obs = got[:, flat + BLOCK :]
    first_block = lax.axis_index("mem") * share
    live_counts = lax.dynamic_slice_in_dim(block_count, first_block, share, 0)
    positions = lax.dynamic_slice_in_dim(obs_offset, first_block, share, 0)
    own_cov = covariances(cross, sum_cells, sum_obs, positions, live_counts, members)
    covariance = gathered_copies(own_cov, "mem", 0)
    correction_delta = apply_cov(covariance, incr_rows)
    returned = correction_delta.reshape(per_region * BLOCK, member_dev)
    return concentration_map + returned.astype(jnp.float32)


def solution(mesh):
    return jax.shard_map(
        per_device,
        mesh=mesh,
        in_specs=(
            P("reg", "mem"),
            P("reg"),
            P("reg", "mem"),
            P("reg", "mem"),
            P("reg", None, None),
            P("reg", None),
            P("reg"),
            P("reg", None),
        ),
        out_specs=P("reg", "mem"),
        check_vma=False,
    )
```

```python
import jax
import jax.numpy as jnp
from jax import lax
from jax.experimental import pallas as pl
from jax.experimental.pallas import tpu as pltpu
from jax.sharding import PartitionSpec as P

BLOCK = 64
KB = 64
STEPS = 4
ROWS = 1024

def advect_kernel(halo_ref, s_ref, x_ref, f_ref, fb_ref, carry_ref):
    @pl.when(pl.program_id(0) == 0)
    def _():
        carry_ref[...] = halo_ref[...]
    x = x_ref[...]
    s = jnp.broadcast_to(s_ref[...], x.shape)
    first = lax.broadcasted_iota(jnp.int32, x.shape, 0) == 0
    last = x.shape[0] - 1
    for k in range(STEPS):
        before = jnp.where(first, carry_ref[k : k + 1, :], pltpu.roll(x, 1, 0))
        carry_ref[k : k + 1, :] = x[last:, :]
        x = x - s * (x - before)
    f_ref[...] = x
    fb_ref[...] = x.astype(jnp.bfloat16)

def advect(halo, speeds, x, interpret=False):
    cells, width = x.shape
    rows = min(ROWS, cells)
    return pl.pallas_call(
        advect_kernel,
        grid=(cells // rows,),
        in_specs=[
            pl.BlockSpec((8, width), lambda t: (0, 0)),
            pl.BlockSpec((rows, 1), lambda t: (t, 0)),
            pl.BlockSpec((rows, width), lambda t: (t, 0)),
        ],
        out_specs=[pl.BlockSpec((rows, width), lambda t: (t, 0)), pl.BlockSpec((rows, width), lambda t: (t, 0))],
        out_shape=[jax.ShapeDtypeStruct(x.shape, jnp.float32), jax.ShapeDtypeStruct(x.shape, jnp.bfloat16)],
        scratch_shapes=[pltpu.VMEM((8, width), jnp.float32)],
        compiler_params=pltpu.CompilerParams(dimension_semantics=("arbitrary",)),
        interpret=interpret,
    )(halo, speeds[:, None], x)

def halo_rows(arrived, arrived_speeds, width):
    v = arrived
    rows = [v[-1]]
    for k in range(1, STEPS):
        v = v[1:] - arrived_speeds[k:, None] * (v[1:] - v[:-1])
        rows.append(v[-1])
    return jnp.concatenate([jnp.stack(rows), jnp.zeros((8 - STEPS, width), v.dtype)], 0)


def passed_along(block, axis, distance):
    devices = range(lax.axis_size(axis))
    route = [((i - distance) % len(devices), i) for i in devices]
    return lax.ppermute(block, axis, route)


def padded(block, sides, width):
    for axis, dim in sides:
        count = lax.axis_size(axis)
        forward = [(i, i + 1) for i in range(count - 1)]
        forward.append((count - 1, 0))
        backward = [(target, source) for source, target in forward]
        low = lax.ppermute(
            lax.slice_in_dim(block, block.shape[dim] - width, None, axis=dim), axis, forward
        )
        high = lax.ppermute(lax.slice_in_dim(block, 0, width, axis=dim), axis, backward)
        block = jnp.concatenate([low, block, high], axis=dim)
    return block


def side_by_side(arrays, axis, dim, along):
    columns = [a.reshape(*a.shape[:along], -1) for a in arrays]
    both = jnp.concatenate(columns, axis=along)
    whole, at, gathered = (lax.psum_scatter(both, axis, scatter_dimension=dim, tiled=True), 0, [])
    for a, column in zip(arrays, columns):
        piece = whole[..., at : at + column.shape[along]]
        gathered.append(piece.reshape(*piece.shape[:along], *a.shape[along:]))
        at += column.shape[along]
    return tuple(gathered)


def laid_out(parts, dim):
    parts = jnp.moveaxis(parts, 0, dim)
    lengths = parts.shape
    return parts.reshape(*lengths[:dim], lengths[dim] * lengths[dim + 1], *lengths[dim + 2 :])


def from_everyone(value, axis):
    copies = jnp.broadcast_to(value, (lax.axis_size(axis), *value.shape))
    return lax.all_to_all(copies, axis, split_axis=0, concat_axis=0, tiled=True)


def gathered_copies(value, axis, dim):
    return laid_out(from_everyone(value, axis), dim)


def taper_mask(positions, live_counts):
    position = jnp.arange(BLOCK).astype(jnp.float32)
    distance = (position[None, :, None] - positions[:, None, :]) / (0.5 * BLOCK)
    active = jnp.arange(KB)[None, :] < live_counts[:, None]
    return jnp.where(active[:, None, :], 1.0 / (1.0 + distance * distance), 0.0)


def block_sums(mesh_point_entries, obs_rows):
    cross = jnp.einsum(
        "bcm,bkm->bck", mesh_point_entries, obs_rows, preferred_element_type=jnp.float32
    )
    sum_cells = jnp.sum(mesh_point_entries.astype(jnp.float32), 2)
    sum_obs = jnp.sum(obs_rows.astype(jnp.float32), 2)
    return (cross, sum_cells, sum_obs)


def covariances(cross, sum_cells, sum_obs, positions, live_counts, members):
    return (
        (cross - sum_cells[:, :, None] * sum_obs[:, None, :] / members)
        / (members - 1)
        * taper_mask(positions, live_counts)
    ).astype(jnp.bfloat16)


def apply_cov(covariance, incr_rows):
    correction_delta = jnp.einsum(
        "bck,bkm->bcm", covariance, incr_rows, preferred_element_type=jnp.float32
    )
    return correction_delta.astype(jnp.bfloat16)


def per_device(
    member_vectors,
    flow_speed_ratio,
    obs_pert,
    obs_incr,
    edge_list,
    block_obs,
    block_count,
    obs_offset,
):
    concentration_map = member_vectors
    outgoing = jnp.concatenate([concentration_map[-STEPS:, :], flow_speed_ratio[-STEPS:, None]], 1)
    arrived = passed_along(outgoing, "reg", 1)
    width = concentration_map.shape[1]
    halo = halo_rows(arrived[:, :-1], arrived[:, -1], width)
    concentration_map, first_guess_state = advect(halo, flow_speed_ratio, concentration_map)
    lend = edge_list.shape[2]
    edge_rows = edge_list.reshape(-1)
    chosen = jnp.stack([obs_pert[edge_rows], obs_incr[edge_rows]])
    rimmed = padded(chosen, (("reg", 1),), lend)
    extended = jnp.concatenate(
        [rimmed[:, :lend], jnp.stack([obs_pert, obs_incr]), rimmed[:, -lend:]], 1
    )
    member_dev = member_vectors.shape[1]
    members = member_dev * lax.axis_size("mem")
    per_region = block_obs.shape[0]
    parts = lax.axis_size("mem")
    pairs = per_region // 2
    share = pairs // parts
    slots = extended.shape[1]
    picks = (block_obs.reshape(-1)[:, None] == jnp.arange(slots)[None, :]).astype(jnp.bfloat16)
    obs_rows = jnp.dot(picks, extended[0], preferred_element_type=jnp.float32).astype(jnp.bfloat16)
    incr_rows = jnp.dot(picks, extended[1], preferred_element_type=jnp.float32).astype(jnp.bfloat16)
    cells_p = first_guess_state.reshape(pairs, 2 * BLOCK, member_dev)
    obs_p = obs_rows.reshape(pairs, 2 * KB, member_dev)
    full = jnp.einsum("brm,blm->brl", cells_p, obs_p, preferred_element_type=jnp.float32)
    upper = (jnp.arange(2 * KB) >= KB)[None, None, :]
    cross = jnp.where(upper, full[:, BLOCK:, :], full[:, :BLOCK, :])
    sum_cells = jnp.sum(first_guess_state.astype(jnp.float32), 1).reshape(pairs, 1, 2 * BLOCK)
    sum_obs = jnp.sum(obs_rows.astype(jnp.float32), 1).reshape(pairs, 1, 2 * KB)
    payload = jnp.concatenate([cross, sum_cells, sum_obs], 1)
    got = lax.psum_scatter(
        payload.reshape(parts, share, BLOCK + 2, 2 * KB), "mem", scatter_dimension=0, tiled=True
    ).reshape(share, BLOCK + 2, 2 * KB)
    cross = got[:, :BLOCK, :]
    cells_sum = jnp.transpose(got[:, BLOCK, :].reshape(share, 2, BLOCK), (0, 2, 1))
    cells_sum = jnp.broadcast_to(cells_sum[:, :, :, None], (share, BLOCK, 2, KB)).reshape(
        share, BLOCK, 2 * KB
    )
    obs_sum = got[:, BLOCK + 1, :][:, None, :]
    first_block = lax.axis_index("mem") * share * 2
    live_counts = lax.dynamic_slice_in_dim(block_count, first_block, share * 2, 0)
    positions = lax.dynamic_slice_in_dim(obs_offset, first_block, share * 2, 0)
    position = jnp.arange(BLOCK).astype(jnp.float32)
    distance = (position[None, :, None] - positions.reshape(share, 1, 2 * KB)) / (0.5 * BLOCK)
    lane = jnp.arange(2 * KB)
    counts = live_counts.reshape(share, 2)[:, lane // KB]
    active = (lane % KB)[None, :] < counts
    taper = jnp.where(active[:, None, :], 1.0 / (1.0 + distance * distance), 0.0)
    own_cov = (
        (cross - cells_sum * obs_sum / members) / (members - 1) * taper
    ).astype(jnp.bfloat16)
    covariance = gathered_copies(own_cov, "mem", 0)
    same_block = (jnp.arange(2 * BLOCK) // BLOCK)[:, None] == (lane // KB)[None, :]
    spread = jnp.where(same_block[None], jnp.concatenate([covariance, covariance], 1), 0)
    incr_p = incr_rows.reshape(pairs, 2 * KB, member_dev)
    correction_delta = jnp.einsum(
        "brl,blm->brm", spread, incr_p, preferred_element_type=jnp.float32
    ).astype(jnp.bfloat16)
    returned = correction_delta.reshape(per_region * BLOCK, member_dev)
    return concentration_map + returned.astype(jnp.float32)


def solution(mesh):
    return jax.shard_map(
        per_device,
        mesh=mesh,
        in_specs=(
            P("reg", "mem"),
            P("reg"),
            P("reg", "mem"),
            P("reg", "mem"),
            P("reg", None, None),
            P("reg", None),
            P("reg"),
            P("reg", None),
        ),
        out_specs=P("reg", "mem"),
        check_vma=False,
    )
```

```python
import jax
import jax.numpy as jnp
from jax import lax
from jax.experimental import pallas as pl
from jax.experimental.pallas import tpu as pltpu
from jax.sharding import PartitionSpec as P

BLOCK = 64
KB = 64
STEPS = 4
ROWS = 1024

def advect_kernel(halo_ref, s_ref, x_ref, f_ref, fb_ref, carry_ref):
    @pl.when(pl.program_id(0) == 0)
    def _():
        carry_ref[...] = halo_ref[...]
    x = x_ref[...]
    lanes = x.shape[1]
    s = jnp.concatenate(
        [jnp.broadcast_to(s_ref[q : q + 1, :], (lanes, lanes)).T for q in range(s_ref.shape[0])], 0
    )
    first = lax.broadcasted_iota(jnp.int32, x.shape, 0) == 0
    last = x.shape[0] - 1
    for k in range(STEPS):
        before = jnp.where(first, carry_ref[k : k + 1, :], pltpu.roll(x, 1, 0))
        carry_ref[k : k + 1, :] = x[last:, :]
        x = x - s * (x - before)
    f_ref[...] = x
    fb_ref[...] = x.astype(jnp.bfloat16)

def advect(halo, speeds, x, interpret=False):
    cells, width = x.shape
    rows = min(ROWS, cells)
    return pl.pallas_call(
        advect_kernel,
        grid=(cells // rows,),
        in_specs=[
            pl.BlockSpec((8, width), lambda t: (0, 0)),
            pl.BlockSpec((rows // width, width), lambda t: (t, 0)),
            pl.BlockSpec((rows, width), lambda t: (t, 0)),
        ],
        out_specs=[pl.BlockSpec((rows, width), lambda t: (t, 0)), pl.BlockSpec((rows, width), lambda t: (t, 0))],
        out_shape=[jax.ShapeDtypeStruct(x.shape, jnp.float32), jax.ShapeDtypeStruct(x.shape, jnp.bfloat16)],
        scratch_shapes=[pltpu.VMEM((8, width), jnp.float32)],
        compiler_params=pltpu.CompilerParams(dimension_semantics=("arbitrary",)),
        interpret=interpret,
    )(halo, speeds.reshape(-1, width), x)

def halo_rows(arrived, arrived_speeds, width):
    v = arrived
    rows = [v[-1]]
    for k in range(1, STEPS):
        v = v[1:] - arrived_speeds[k:, None] * (v[1:] - v[:-1])
        rows.append(v[-1])
    return jnp.concatenate([jnp.stack(rows), jnp.zeros((8 - STEPS, width), v.dtype)], 0)


def passed_along(block, axis, distance):
    devices = range(lax.axis_size(axis))
    route = [((i - distance) % len(devices), i) for i in devices]
    return lax.ppermute(block, axis, route)


def padded(block, sides, width):
    for axis, dim in sides:
        count = lax.axis_size(axis)
        forward = [(i, i + 1) for i in range(count - 1)]
        forward.append((count - 1, 0))
        backward = [(target, source) for source, target in forward]
        low = lax.ppermute(
            lax.slice_in_dim(block, block.shape[dim] - width, None, axis=dim), axis, forward
        )
        high = lax.ppermute(lax.slice_in_dim(block, 0, width, axis=dim), axis, backward)
        block = jnp.concatenate([low, block, high], axis=dim)
    return block


def side_by_side(arrays, axis, dim, along):
    columns = [a.reshape(*a.shape[:along], -1) for a in arrays]
    both = jnp.concatenate(columns, axis=along)
    whole, at, gathered = (lax.psum_scatter(both, axis, scatter_dimension=dim, tiled=True), 0, [])
    for a, column in zip(arrays, columns):
        piece = whole[..., at : at + column.shape[along]]
        gathered.append(piece.reshape(*piece.shape[:along], *a.shape[along:]))
        at += column.shape[along]
    return tuple(gathered)


def laid_out(parts, dim):
    parts = jnp.moveaxis(parts, 0, dim)
    lengths = parts.shape
    return parts.reshape(*lengths[:dim], lengths[dim] * lengths[dim + 1], *lengths[dim + 2 :])


def from_everyone(value, axis):
    copies = jnp.broadcast_to(value, (lax.axis_size(axis), *value.shape))
    return lax.all_to_all(copies, axis, split_axis=0, concat_axis=0, tiled=True)


def gathered_copies(value, axis, dim):
    return laid_out(from_everyone(value, axis), dim)


def taper_mask(positions, live_counts):
    position = jnp.arange(BLOCK).astype(jnp.float32)
    distance = (position[None, :, None] - positions[:, None, :]) / (0.5 * BLOCK)
    active = jnp.arange(KB)[None, :] < live_counts[:, None]
    return jnp.where(active[:, None, :], 1.0 / (1.0 + distance * distance), 0.0)


def block_sums(mesh_point_entries, obs_rows):
    cross = jnp.einsum(
        "bcm,bkm->bck", mesh_point_entries, obs_rows, preferred_element_type=jnp.float32
    )
    sum_cells = jnp.sum(mesh_point_entries.astype(jnp.float32), 2)
    sum_obs = jnp.sum(obs_rows.astype(jnp.float32), 2)
    return (cross, sum_cells, sum_obs)


def covariances(cross, sum_cells, sum_obs, positions, live_counts, members):
    return (
        (cross - sum_cells[:, :, None] * sum_obs[:, None, :] / members)
        / (members - 1)
        * taper_mask(positions, live_counts)
    ).astype(jnp.bfloat16)


def apply_cov(covariance, incr_rows):
    correction_delta = jnp.einsum(
        "bck,bkm->bcm", covariance, incr_rows, preferred_element_type=jnp.float32
    )
    return correction_delta.astype(jnp.bfloat16)


def per_device(
    member_vectors,
    flow_speed_ratio,
    obs_pert,
    obs_incr,
    edge_list,
    block_obs,
    block_count,
    obs_offset,
):
    concentration_map = member_vectors
    outgoing = jnp.concatenate([concentration_map[-STEPS:, :], flow_speed_ratio[-STEPS:, None]], 1)
    arrived = passed_along(outgoing, "reg", 1)
    width = concentration_map.shape[1]
    halo = halo_rows(arrived[:, :-1], arrived[:, -1], width)
    concentration_map, first_guess_state = advect(halo, flow_speed_ratio, concentration_map)
    lend = edge_list.shape[2]
    edge_rows = edge_list.reshape(-1)
    own = obs_pert.shape[0]
    lent = (edge_rows[:, None] == jnp.arange(own)[None, :]).astype(jnp.bfloat16)
    chosen = jnp.stack(
        [
            jnp.dot(lent, obs_pert, preferred_element_type=jnp.float32).astype(jnp.bfloat16),
            jnp.dot(lent, obs_incr, preferred_element_type=jnp.float32).astype(jnp.bfloat16),
        ]
    )
    rimmed = padded(chosen, (("reg", 1),), lend)
    extended = jnp.concatenate(
        [rimmed[:, :lend], jnp.stack([obs_pert, obs_incr]), rimmed[:, -lend:]], 1
    )
    member_dev = member_vectors.shape[1]
    members = member_dev * lax.axis_size("mem")
    per_region = block_obs.shape[0]
    parts = lax.axis_size("mem")
    pairs = per_region // 2
    share = pairs // parts
    slots = extended.shape[1]
    picks = (block_obs.reshape(-1)[:, None] == jnp.arange(slots)[None, :]).astype(jnp.bfloat16)
    obs_rows = jnp.dot(picks, extended[0], preferred_element_type=jnp.float32).astype(jnp.bfloat16)
    incr_rows = jnp.dot(picks, extended[1], preferred_element_type=jnp.float32).astype(jnp.bfloat16)
    cells_p = first_guess_state.reshape(pairs, 2 * BLOCK, member_dev)
    obs_p = obs_rows.reshape(pairs, 2 * KB, member_dev)
    full = jnp.einsum("brm,blm->brl", cells_p, obs_p, preferred_element_type=jnp.float32)
    upper = (jnp.arange(2 * KB) >= KB)[None, None, :]
    cross = jnp.where(upper, full[:, BLOCK:, :], full[:, :BLOCK, :])
    sum_cells = jnp.sum(first_guess_state.astype(jnp.float32), 1).reshape(pairs, 1, 2 * BLOCK)
    sum_obs = jnp.sum(obs_rows.astype(jnp.float32), 1).reshape(pairs, 1, 2 * KB)
    payload = jnp.concatenate([cross, sum_cells, sum_obs], 1)
    got = lax.psum_scatter(
        payload.reshape(parts, share, BLOCK + 2, 2 * KB), "mem", scatter_dimension=0, tiled=True
    ).reshape(share, BLOCK + 2, 2 * KB)
    cross = got[:, :BLOCK, :]
    cells_sum = jnp.transpose(got[:, BLOCK, :].reshape(share, 2, BLOCK), (0, 2, 1))
    cells_sum = jnp.broadcast_to(cells_sum[:, :, :, None], (share, BLOCK, 2, KB)).reshape(
        share, BLOCK, 2 * KB
    )
    obs_sum = got[:, BLOCK + 1, :][:, None, :]
    first_block = lax.axis_index("mem") * share * 2
    live_counts = lax.dynamic_slice_in_dim(block_count, first_block, share * 2, 0)
    positions = lax.dynamic_slice_in_dim(obs_offset, first_block, share * 2, 0)
    position = jnp.arange(BLOCK).astype(jnp.float32)
    distance = (position[None, :, None] - positions.reshape(share, 1, 2 * KB)) / (0.5 * BLOCK)
    lane = jnp.arange(2 * KB)
    counts = live_counts.reshape(share, 2)[:, lane // KB]
    active = (lane % KB)[None, :] < counts
    taper = jnp.where(active[:, None, :], 1.0 / (1.0 + distance * distance), 0.0)
    own_cov = (
        (cross - cells_sum * obs_sum / members) / (members - 1) * taper
    ).astype(jnp.bfloat16)
    covariance = gathered_copies(own_cov, "mem", 0)
    same_block = (jnp.arange(2 * BLOCK) // BLOCK)[:, None] == (lane // KB)[None, :]
    spread = jnp.where(same_block[None], jnp.concatenate([covariance, covariance], 1), 0)
    incr_p = incr_rows.reshape(pairs, 2 * KB, member_dev)
    correction_delta = jnp.einsum(
        "brl,blm->brm", spread, incr_p, preferred_element_type=jnp.float32
    ).astype(jnp.bfloat16)
    returned = correction_delta.reshape(per_region * BLOCK, member_dev)
    return concentration_map + returned.astype(jnp.float32)


def solution(mesh):
    return jax.shard_map(
        per_device,
        mesh=mesh,
        in_specs=(
            P("reg", "mem"),
            P("reg"),
            P("reg", "mem"),
            P("reg", "mem"),
            P("reg", None, None),
            P("reg", None),
            P("reg"),
            P("reg", None),
        ),
        out_specs=P("reg", "mem"),
        check_vma=False,
    )
```

```python
import jax
import jax.numpy as jnp
from jax import lax
from jax.experimental import pallas as pl
from jax.experimental.pallas import tpu as pltpu
from jax.sharding import Mesh, PartitionSpec as P

BLOCK = 64
KB = 64
STEPS = 4
ROWS = 1024
CORES = 2
MEM = ("z", "core")

def advect_kernel(halo_ref, s_ref, x_ref, f_ref, fb_ref, carry_ref):
    @pl.when(pl.program_id(0) == 0)
    def _():
        carry_ref[...] = halo_ref[...]
    x = x_ref[...]
    lanes = x.shape[1]
    s = jnp.concatenate(
        [jnp.broadcast_to(s_ref[q : q + 1, :], (lanes, lanes)).T for q in range(s_ref.shape[0])], 0
    )
    first = lax.broadcasted_iota(jnp.int32, x.shape, 0) == 0
    last = x.shape[0] - 1
    for k in range(STEPS):
        before = jnp.where(first, carry_ref[k : k + 1, :], pltpu.roll(x, 1, 0))
        carry_ref[k : k + 1, :] = x[last:, :]
        x = x - s * (x - before)
    f_ref[...] = x
    fb_ref[...] = x.astype(jnp.bfloat16)

def advect(halo, speeds, x, interpret=False):
    cells, width = x.shape
    rows = min(ROWS, cells)
    return pl.pallas_call(
        advect_kernel,
        grid=(cells // rows,),
        in_specs=[
            pl.BlockSpec((8, width), lambda t: (0, 0)),
            pl.BlockSpec((rows // width, width), lambda t: (t, 0)),
            pl.BlockSpec((rows, width), lambda t: (t, 0)),
        ],
        out_specs=[pl.BlockSpec((rows, width), lambda t: (t, 0)), pl.BlockSpec((rows, width), lambda t: (t, 0))],
        out_shape=[jax.ShapeDtypeStruct(x.shape, jnp.float32), jax.ShapeDtypeStruct(x.shape, jnp.bfloat16)],
        scratch_shapes=[pltpu.VMEM((8, width), jnp.float32)],
        compiler_params=pltpu.CompilerParams(dimension_semantics=("arbitrary",)),
        interpret=interpret,
    )(halo, speeds.reshape(-1, width), x)

def halo_rows(arrived, arrived_speeds, width):
    v = arrived
    rows = [v[-1]]
    for k in range(1, STEPS):
        v = v[1:] - arrived_speeds[k:, None] * (v[1:] - v[:-1])
        rows.append(v[-1])
    return jnp.concatenate([jnp.stack(rows), jnp.zeros((8 - STEPS, width), v.dtype)], 0)


def passed_along(block, axis, distance):
    devices = range(lax.axis_size(axis))
    route = [((i - distance) % len(devices), i) for i in devices]
    return lax.ppermute(block, axis, route)


def padded(block, sides, width):
    for axis, dim in sides:
        count = lax.axis_size(axis)
        forward = [(i, i + 1) for i in range(count - 1)]
        forward.append((count - 1, 0))
        backward = [(target, source) for source, target in forward]
        low = lax.ppermute(
            lax.slice_in_dim(block, block.shape[dim] - width, None, axis=dim), axis, forward
        )
        high = lax.ppermute(lax.slice_in_dim(block, 0, width, axis=dim), axis, backward)
        block = jnp.concatenate([low, block, high], axis=dim)
    return block


def side_by_side(arrays, axis, dim, along):
    columns = [a.reshape(*a.shape[:along], -1) for a in arrays]
    both = jnp.concatenate(columns, axis=along)
    whole, at, gathered = (lax.psum_scatter(both, axis, scatter_dimension=dim, tiled=True), 0, [])
    for a, column in zip(arrays, columns):
        piece = whole[..., at : at + column.shape[along]]
        gathered.append(piece.reshape(*piece.shape[:along], *a.shape[along:]))
        at += column.shape[along]
    return tuple(gathered)


def laid_out(parts, dim):
    parts = jnp.moveaxis(parts, 0, dim)
    lengths = parts.shape
    return parts.reshape(*lengths[:dim], lengths[dim] * lengths[dim + 1], *lengths[dim + 2 :])


def from_everyone(value, axis):
    copies = jnp.broadcast_to(value, (lax.axis_size(axis), *value.shape))
    return lax.all_to_all(copies, axis, split_axis=0, concat_axis=0, tiled=True)


def gathered_copies(value, axis, dim):
    chips, cores = lax.axis_size("z"), lax.axis_size("core")
    along_z = lax.all_to_all(
        jnp.broadcast_to(value, (chips, *value.shape)), "z", split_axis=0, concat_axis=0, tiled=True
    )
    both = lax.all_to_all(
        jnp.broadcast_to(along_z, (cores, *along_z.shape)), "core", split_axis=0, concat_axis=0, tiled=True
    )
    return laid_out(jnp.swapaxes(both, 0, 1).reshape(chips * cores, *value.shape), dim)


def taper_mask(positions, live_counts):
    position = jnp.arange(BLOCK).astype(jnp.float32)
    distance = (position[None, :, None] - positions[:, None, :]) / (0.5 * BLOCK)
    active = jnp.arange(KB)[None, :] < live_counts[:, None]
    return jnp.where(active[:, None, :], 1.0 / (1.0 + distance * distance), 0.0)


def block_sums(mesh_point_entries, obs_rows):
    cross = jnp.einsum(
        "bcm,bkm->bck", mesh_point_entries, obs_rows, preferred_element_type=jnp.float32
    )
    sum_cells = jnp.sum(mesh_point_entries.astype(jnp.float32), 2)
    sum_obs = jnp.sum(obs_rows.astype(jnp.float32), 2)
    return (cross, sum_cells, sum_obs)


def covariances(cross, sum_cells, sum_obs, positions, live_counts, members):
    return (
        (cross - sum_cells[:, :, None] * sum_obs[:, None, :] / members)
        / (members - 1)
        * taper_mask(positions, live_counts)
    ).astype(jnp.bfloat16)


def apply_cov(covariance, incr_rows):
    correction_delta = jnp.einsum(
        "bck,bkm->bcm", covariance, incr_rows, preferred_element_type=jnp.float32
    )
    return correction_delta.astype(jnp.bfloat16)


def per_device(
    member_vectors,
    flow_speed_ratio,
    obs_pert,
    obs_incr,
    edge_list,
    block_obs,
    block_count,
    obs_offset,
):
    concentration_map = member_vectors
    outgoing = jnp.concatenate([concentration_map[-STEPS:, :], flow_speed_ratio[-STEPS:, None]], 1)
    arrived = passed_along(outgoing, "reg", 1)
    width = concentration_map.shape[1]
    halo = halo_rows(arrived[:, :-1], arrived[:, -1], width)
    concentration_map, first_guess_state = advect(halo, flow_speed_ratio, concentration_map)
    lend = edge_list.shape[2]
    edge_rows = edge_list.reshape(-1)
    own = obs_pert.shape[0]
    lent = (edge_rows[:, None] == jnp.arange(own)[None, :]).astype(jnp.bfloat16)
    chosen = jnp.stack(
        [
            jnp.dot(lent, obs_pert, preferred_element_type=jnp.float32).astype(jnp.bfloat16),
            jnp.dot(lent, obs_incr, preferred_element_type=jnp.float32).astype(jnp.bfloat16),
        ]
    )
    rimmed = padded(chosen, (("reg", 1),), lend)
    extended = jnp.concatenate(
        [rimmed[:, :lend], jnp.stack([obs_pert, obs_incr]), rimmed[:, -lend:]], 1
    )
    member_dev = member_vectors.shape[1]
    members = member_dev * lax.axis_size(MEM)
    per_region = block_obs.shape[0]
    parts = lax.axis_size(MEM)
    pairs = per_region // 2
    share = pairs // parts
    slots = extended.shape[1]
    picks = (block_obs.reshape(-1)[:, None] == jnp.arange(slots)[None, :]).astype(jnp.bfloat16)
    obs_rows = jnp.dot(picks, extended[0], preferred_element_type=jnp.float32).astype(jnp.bfloat16)
    incr_rows = jnp.dot(picks, extended[1], preferred_element_type=jnp.float32).astype(jnp.bfloat16)
    cells_p = first_guess_state.reshape(pairs, 2 * BLOCK, member_dev)
    obs_p = obs_rows.reshape(pairs, 2 * KB, member_dev)
    full = jnp.einsum("brm,blm->brl", cells_p, obs_p, preferred_element_type=jnp.float32)
    upper = (jnp.arange(2 * KB) >= KB)[None, None, :]
    cross = jnp.where(upper, full[:, BLOCK:, :], full[:, :BLOCK, :])
    sum_cells = jnp.sum(first_guess_state.astype(jnp.float32), 1).reshape(pairs, 1, 2 * BLOCK)
    sum_obs = jnp.sum(obs_rows.astype(jnp.float32), 1).reshape(pairs, 1, 2 * KB)
    payload = jnp.concatenate([cross, sum_cells, sum_obs], 1)
    got = lax.psum_scatter(
        payload.reshape(parts, share, BLOCK + 2, 2 * KB), MEM, scatter_dimension=0, tiled=True
    ).reshape(share, BLOCK + 2, 2 * KB)
    cross = got[:, :BLOCK, :]
    cells_sum = jnp.transpose(got[:, BLOCK, :].reshape(share, 2, BLOCK), (0, 2, 1))
    cells_sum = jnp.broadcast_to(cells_sum[:, :, :, None], (share, BLOCK, 2, KB)).reshape(
        share, BLOCK, 2 * KB
    )
    obs_sum = got[:, BLOCK + 1, :][:, None, :]
    first_block = lax.axis_index(MEM) * share * 2
    live_counts = lax.dynamic_slice_in_dim(block_count, first_block, share * 2, 0)
    positions = lax.dynamic_slice_in_dim(obs_offset, first_block, share * 2, 0)
    position = jnp.arange(BLOCK).astype(jnp.float32)
    distance = (position[None, :, None] - positions.reshape(share, 1, 2 * KB)) / (0.5 * BLOCK)
    lane = jnp.arange(2 * KB)
    counts = live_counts.reshape(share, 2)[:, lane // KB]
    active = (lane % KB)[None, :] < counts
    taper = jnp.where(active[:, None, :], 1.0 / (1.0 + distance * distance), 0.0)
    own_cov = (
        (cross - cells_sum * obs_sum / members) / (members - 1) * taper
    ).astype(jnp.bfloat16)
    covariance = gathered_copies(own_cov, MEM, 0)
    same_block = (jnp.arange(2 * BLOCK) // BLOCK)[:, None] == (lane // KB)[None, :]
    spread = jnp.where(same_block[None], jnp.concatenate([covariance, covariance], 1), 0)
    incr_p = incr_rows.reshape(pairs, 2 * KB, member_dev)
    correction_delta = jnp.einsum(
        "brl,blm->brm", spread, incr_p, preferred_element_type=jnp.float32
    ).astype(jnp.bfloat16)
    returned = correction_delta.reshape(per_region * BLOCK, member_dev)
    return concentration_map + returned.astype(jnp.float32)


def solution(mesh):
    mem, reg = mesh.devices.shape
    split = Mesh(mesh.devices.reshape(mem // CORES, CORES, reg), ("z", "core", "reg"))
    return jax.shard_map(
        per_device,
        mesh=split,
        in_specs=(
            P("reg", MEM),
            P("reg"),
            P("reg", MEM),
            P("reg", MEM),
            P("reg", None, None),
            P("reg", None),
            P("reg"),
            P("reg", None),
        ),
        out_specs=P("reg", MEM),
        check_vma=False,
    )
```

```python
import jax
import jax.numpy as jnp
from jax import lax
from jax.experimental import pallas as pl
from jax.experimental.pallas import tpu as pltpu
from jax.sharding import Mesh, PartitionSpec as P

BLOCK = 64
KB = 64
STEPS = 4
ROWS = 2048
CORES = 2
MEM = ("z", "core")

def advect_kernel(halo_ref, s_ref, x_ref, f_ref, fb_ref, carry_ref):
    @pl.when(pl.program_id(0) == 0)
    def _():
        carry_ref[...] = halo_ref[...]
    x = x_ref[...]
    lanes = x.shape[1]
    s = jnp.concatenate(
        [jnp.broadcast_to(s_ref[q : q + 1, :], (lanes, lanes)).T for q in range(s_ref.shape[0])], 0
    )
    first = lax.broadcasted_iota(jnp.int32, x.shape, 0) == 0
    last = x.shape[0] - 1
    for k in range(STEPS):
        before = jnp.where(first, carry_ref[k : k + 1, :], pltpu.roll(x, 1, 0))
        carry_ref[k : k + 1, :] = x[last:, :]
        x = x - s * (x - before)
    f_ref[...] = x
    fb_ref[...] = x.astype(jnp.bfloat16)

def advect(halo, speeds, x, interpret=False):
    cells, width = x.shape
    rows = min(ROWS, cells)
    return pl.pallas_call(
        advect_kernel,
        grid=(cells // rows,),
        in_specs=[
            pl.BlockSpec((8, width), lambda t: (0, 0)),
            pl.BlockSpec((rows // width, width), lambda t: (t, 0)),
            pl.BlockSpec((rows, width), lambda t: (t, 0)),
        ],
        out_specs=[pl.BlockSpec((rows, width), lambda t: (t, 0)), pl.BlockSpec((rows, width), lambda t: (t, 0))],
        out_shape=[jax.ShapeDtypeStruct(x.shape, jnp.float32), jax.ShapeDtypeStruct(x.shape, jnp.bfloat16)],
        scratch_shapes=[pltpu.VMEM((8, width), jnp.float32)],
        compiler_params=pltpu.CompilerParams(dimension_semantics=("arbitrary",)),
        interpret=interpret,
    )(halo, speeds.reshape(-1, width), x)

def halo_rows(arrived, arrived_speeds, width):
    v = arrived
    rows = [v[-1]]
    for k in range(1, STEPS):
        v = v[1:] - arrived_speeds[k:, None] * (v[1:] - v[:-1])
        rows.append(v[-1])
    return jnp.concatenate([jnp.stack(rows), jnp.zeros((8 - STEPS, width), v.dtype)], 0)


def passed_along(block, axis, distance):
    devices = range(lax.axis_size(axis))
    route = [((i - distance) % len(devices), i) for i in devices]
    return lax.ppermute(block, axis, route)


def padded(block, sides, width):
    for axis, dim in sides:
        count = lax.axis_size(axis)
        forward = [(i, i + 1) for i in range(count - 1)]
        forward.append((count - 1, 0))
        backward = [(target, source) for source, target in forward]
        low = lax.ppermute(
            lax.slice_in_dim(block, block.shape[dim] - width, None, axis=dim), axis, forward
        )
        high = lax.ppermute(lax.slice_in_dim(block, 0, width, axis=dim), axis, backward)
        block = jnp.concatenate([low, block, high], axis=dim)
    return block


def side_by_side(arrays, axis, dim, along):
    columns = [a.reshape(*a.shape[:along], -1) for a in arrays]
    both = jnp.concatenate(columns, axis=along)
    whole, at, gathered = (lax.psum_scatter(both, axis, scatter_dimension=dim, tiled=True), 0, [])
    for a, column in zip(arrays, columns):
        piece = whole[..., at : at + column.shape[along]]
        gathered.append(piece.reshape(*piece.shape[:along], *a.shape[along:]))
        at += column.shape[along]
    return tuple(gathered)


def laid_out(parts, dim):
    parts = jnp.moveaxis(parts, 0, dim)
    lengths = parts.shape
    return parts.reshape(*lengths[:dim], lengths[dim] * lengths[dim + 1], *lengths[dim + 2 :])


def from_everyone(value, axis):
    copies = jnp.broadcast_to(value, (lax.axis_size(axis), *value.shape))
    return lax.all_to_all(copies, axis, split_axis=0, concat_axis=0, tiled=True)


def gathered_copies(value, axis, dim):
    chips, cores = lax.axis_size("z"), lax.axis_size("core")
    along_z = lax.all_to_all(
        jnp.broadcast_to(value, (chips, *value.shape)), "z", split_axis=0, concat_axis=0, tiled=True
    )
    both = lax.all_to_all(
        jnp.broadcast_to(along_z, (cores, *along_z.shape)), "core", split_axis=0, concat_axis=0, tiled=True
    )
    return laid_out(jnp.swapaxes(both, 0, 1).reshape(chips * cores, *value.shape), dim)


def taper_mask(positions, live_counts):
    position = jnp.arange(BLOCK).astype(jnp.float32)
    distance = (position[None, :, None] - positions[:, None, :]) / (0.5 * BLOCK)
    active = jnp.arange(KB)[None, :] < live_counts[:, None]
    return jnp.where(active[:, None, :], 1.0 / (1.0 + distance * distance), 0.0)


def block_sums(mesh_point_entries, obs_rows):
    cross = jnp.einsum(
        "bcm,bkm->bck", mesh_point_entries, obs_rows, preferred_element_type=jnp.float32
    )
    sum_cells = jnp.sum(mesh_point_entries.astype(jnp.float32), 2)
    sum_obs = jnp.sum(obs_rows.astype(jnp.float32), 2)
    return (cross, sum_cells, sum_obs)


def covariances(cross, sum_cells, sum_obs, positions, live_counts, members):
    return (
        (cross - sum_cells[:, :, None] * sum_obs[:, None, :] / members)
        / (members - 1)
        * taper_mask(positions, live_counts)
    ).astype(jnp.bfloat16)


def apply_cov(covariance, incr_rows):
    correction_delta = jnp.einsum(
        "bck,bkm->bcm", covariance, incr_rows, preferred_element_type=jnp.float32
    )
    return correction_delta.astype(jnp.bfloat16)


def per_device(
    member_vectors,
    flow_speed_ratio,
    obs_pert,
    obs_incr,
    edge_list,
    block_obs,
    block_count,
    obs_offset,
):
    concentration_map = member_vectors
    outgoing = jnp.concatenate([concentration_map[-STEPS:, :], flow_speed_ratio[-STEPS:, None]], 1)
    arrived = passed_along(outgoing, "reg", 1)
    width = concentration_map.shape[1]
    halo = halo_rows(arrived[:, :-1], arrived[:, -1], width)
    concentration_map, first_guess_state = advect(halo, flow_speed_ratio, concentration_map)
    lend = edge_list.shape[2]
    edge_rows = edge_list.reshape(-1)
    own = obs_pert.shape[0]
    lent = (edge_rows[:, None] == jnp.arange(own)[None, :]).astype(jnp.bfloat16)
    chosen = jnp.stack(
        [
            jnp.dot(lent, obs_pert, preferred_element_type=jnp.float32).astype(jnp.bfloat16),
            jnp.dot(lent, obs_incr, preferred_element_type=jnp.float32).astype(jnp.bfloat16),
        ]
    )
    rimmed = padded(chosen, (("reg", 1),), lend)
    extended = jnp.concatenate(
        [rimmed[:, :lend], jnp.stack([obs_pert, obs_incr]), rimmed[:, -lend:]], 1
    )
    member_dev = member_vectors.shape[1]
    members = member_dev * lax.axis_size(MEM)
    per_region = block_obs.shape[0]
    parts = lax.axis_size(MEM)
    pairs = per_region // 2
    share = pairs // parts
    slots = extended.shape[1]
    picks = (block_obs.reshape(-1)[:, None] == jnp.arange(slots)[None, :]).astype(jnp.bfloat16)
    obs_rows = jnp.dot(picks, extended[0], preferred_element_type=jnp.float32).astype(jnp.bfloat16)
    incr_rows = jnp.dot(picks, extended[1], preferred_element_type=jnp.float32).astype(jnp.bfloat16)
    cells_p = first_guess_state.reshape(pairs, 2 * BLOCK, member_dev)
    obs_p = obs_rows.reshape(pairs, 2 * KB, member_dev)
    full = jnp.einsum("brm,blm->brl", cells_p, obs_p, preferred_element_type=jnp.float32)
    upper = (jnp.arange(2 * KB) >= KB)[None, None, :]
    cross = jnp.where(upper, full[:, BLOCK:, :], full[:, :BLOCK, :])
    sum_cells = jnp.sum(first_guess_state.astype(jnp.float32), 1).reshape(pairs, 1, 2 * BLOCK)
    table_sums = jnp.sum(extended[0].astype(jnp.float32), 1)
    sum_obs = table_sums[block_obs].reshape(pairs, 1, 2 * KB)
    payload = jnp.concatenate([cross, sum_cells, sum_obs], 1)
    got = lax.psum_scatter(
        payload.reshape(parts, share, BLOCK + 2, 2 * KB), MEM, scatter_dimension=0, tiled=True
    ).reshape(share, BLOCK + 2, 2 * KB)
    cross = got[:, :BLOCK, :]
    cells_sum = jnp.transpose(got[:, BLOCK, :].reshape(share, 2, BLOCK), (0, 2, 1))
    cells_sum = jnp.broadcast_to(cells_sum[:, :, :, None], (share, BLOCK, 2, KB)).reshape(
        share, BLOCK, 2 * KB
    )
    obs_sum = got[:, BLOCK + 1, :][:, None, :]
    first_block = lax.axis_index(MEM) * share * 2
    live_counts = lax.dynamic_slice_in_dim(block_count, first_block, share * 2, 0)
    positions = lax.dynamic_slice_in_dim(obs_offset, first_block, share * 2, 0)
    position = jnp.arange(BLOCK).astype(jnp.float32)
    distance = (position[None, :, None] - positions.reshape(share, 1, 2 * KB)) / (0.5 * BLOCK)
    lane = jnp.arange(2 * KB)
    counts = live_counts.reshape(share, 2)[:, lane // KB]
    active = (lane % KB)[None, :] < counts
    taper = jnp.where(active[:, None, :], 1.0 / (1.0 + distance * distance), 0.0)
    own_cov = (
        (cross - cells_sum * obs_sum / members) / (members - 1) * taper
    ).astype(jnp.bfloat16)
    covariance = gathered_copies(own_cov, MEM, 0)
    same_block = (jnp.arange(2 * BLOCK) // BLOCK)[:, None] == (lane // KB)[None, :]
    spread = jnp.where(same_block[None], jnp.concatenate([covariance, covariance], 1), 0)
    incr_p = incr_rows.reshape(pairs, 2 * KB, member_dev)
    correction_delta = jnp.einsum(
        "brl,blm->brm", spread, incr_p, preferred_element_type=jnp.float32
    ).astype(jnp.bfloat16)
    returned = correction_delta.reshape(per_region * BLOCK, member_dev)
    return concentration_map + returned.astype(jnp.float32)


def solution(mesh):
    mem, reg = mesh.devices.shape
    split = Mesh(mesh.devices.reshape(mem // CORES, CORES, reg), ("z", "core", "reg"))
    return jax.shard_map(
        per_device,
        mesh=split,
        in_specs=(
            P("reg", MEM),
            P("reg"),
            P("reg", MEM),
            P("reg", MEM),
            P("reg", None, None),
            P("reg", None),
            P("reg"),
            P("reg", None),
        ),
        out_specs=P("reg", MEM),
        check_vma=False,
    )
```

```python
import jax
import jax.numpy as jnp
from jax import lax
from jax.experimental import pallas as pl
from jax.experimental.pallas import tpu as pltpu
from jax.sharding import Mesh, PartitionSpec as P

BLOCK = 64
KB = 64
STEPS = 4
ROWS = 2048
CORES = 2
MEM = ("z", "core")

def advect_kernel(halo_ref, s_ref, x_ref, f_ref, fb_ref, carry_ref):
    @pl.when(pl.program_id(0) == 0)
    def _():
        carry_ref[...] = halo_ref[...]
    x = x_ref[...]
    lanes = x.shape[1]
    s = jnp.concatenate(
        [jnp.broadcast_to(s_ref[q : q + 1, :], (lanes, lanes)).T for q in range(s_ref.shape[0])], 0
    )
    first = lax.broadcasted_iota(jnp.int32, x.shape, 0) == 0
    last = x.shape[0] - 1
    for k in range(STEPS):
        before = jnp.where(first, carry_ref[k : k + 1, :], pltpu.roll(x, 1, 0))
        carry_ref[k : k + 1, :] = x[last:, :]
        x = x - s * (x - before)
    f_ref[...] = x
    fb_ref[...] = x.astype(jnp.bfloat16)

def advect(halo, speeds, x, interpret=False):
    cells, width = x.shape
    rows = min(ROWS, cells)
    return pl.pallas_call(
        advect_kernel,
        grid=(cells // rows,),
        in_specs=[
            pl.BlockSpec((8, width), lambda t: (0, 0)),
            pl.BlockSpec((rows // width, width), lambda t: (t, 0)),
            pl.BlockSpec((rows, width), lambda t: (t, 0)),
        ],
        out_specs=[pl.BlockSpec((rows, width), lambda t: (t, 0)), pl.BlockSpec((rows, width), lambda t: (t, 0))],
        out_shape=[jax.ShapeDtypeStruct(x.shape, jnp.float32), jax.ShapeDtypeStruct(x.shape, jnp.bfloat16)],
        scratch_shapes=[pltpu.VMEM((8, width), jnp.float32)],
        compiler_params=pltpu.CompilerParams(dimension_semantics=("arbitrary",)),
        interpret=interpret,
    )(halo, speeds.reshape(-1, width), x)

def halo_rows(arrived, arrived_speeds, width):
    v = arrived
    rows = [v[-1]]
    for k in range(1, STEPS):
        v = v[1:] - arrived_speeds[k:, None] * (v[1:] - v[:-1])
        rows.append(v[-1])
    return jnp.concatenate([jnp.stack(rows), jnp.zeros((8 - STEPS, width), v.dtype)], 0)


def passed_along(block, axis, distance):
    devices = range(lax.axis_size(axis))
    route = [((i - distance) % len(devices), i) for i in devices]
    return lax.ppermute(block, axis, route)


def padded(block, sides, width):
    for axis, dim in sides:
        count = lax.axis_size(axis)
        forward = [(i, i + 1) for i in range(count - 1)]
        forward.append((count - 1, 0))
        backward = [(target, source) for source, target in forward]
        low = lax.ppermute(
            lax.slice_in_dim(block, block.shape[dim] - width, None, axis=dim), axis, forward
        )
        high = lax.ppermute(lax.slice_in_dim(block, 0, width, axis=dim), axis, backward)
        block = jnp.concatenate([low, block, high], axis=dim)
    return block


def side_by_side(arrays, axis, dim, along):
    columns = [a.reshape(*a.shape[:along], -1) for a in arrays]
    both = jnp.concatenate(columns, axis=along)
    whole, at, gathered = (lax.psum_scatter(both, axis, scatter_dimension=dim, tiled=True), 0, [])
    for a, column in zip(arrays, columns):
        piece = whole[..., at : at + column.shape[along]]
        gathered.append(piece.reshape(*piece.shape[:along], *a.shape[along:]))
        at += column.shape[along]
    return tuple(gathered)


def laid_out(parts, dim):
    parts = jnp.moveaxis(parts, 0, dim)
    lengths = parts.shape
    return parts.reshape(*lengths[:dim], lengths[dim] * lengths[dim + 1], *lengths[dim + 2 :])


def from_everyone(value, axis):
    copies = jnp.broadcast_to(value, (lax.axis_size(axis), *value.shape))
    return lax.all_to_all(copies, axis, split_axis=0, concat_axis=0, tiled=True)


def gathered_copies(value, axis, dim):
    chips, cores = lax.axis_size("z"), lax.axis_size("core")
    along_z = lax.all_to_all(
        jnp.broadcast_to(value, (chips, *value.shape)), "z", split_axis=0, concat_axis=0, tiled=True
    )
    both = lax.all_to_all(
        jnp.broadcast_to(along_z, (cores, *along_z.shape)), "core", split_axis=0, concat_axis=0, tiled=True
    )
    return laid_out(jnp.swapaxes(both, 0, 1).reshape(chips * cores, *value.shape), dim)


def taper_mask(positions, live_counts):
    position = jnp.arange(BLOCK).astype(jnp.float32)
    distance = (position[None, :, None] - positions[:, None, :]) / (0.5 * BLOCK)
    active = jnp.arange(KB)[None, :] < live_counts[:, None]
    return jnp.where(active[:, None, :], 1.0 / (1.0 + distance * distance), 0.0)


def block_sums(mesh_point_entries, obs_rows):
    cross = jnp.einsum(
        "bcm,bkm->bck", mesh_point_entries, obs_rows, preferred_element_type=jnp.float32
    )
    sum_cells = jnp.sum(mesh_point_entries.astype(jnp.float32), 2)
    sum_obs = jnp.sum(obs_rows.astype(jnp.float32), 2)
    return (cross, sum_cells, sum_obs)


def covariances(cross, sum_cells, sum_obs, positions, live_counts, members):
    return (
        (cross - sum_cells[:, :, None] * sum_obs[:, None, :] / members)
        / (members - 1)
        * taper_mask(positions, live_counts)
    ).astype(jnp.bfloat16)


def apply_cov(covariance, incr_rows):
    correction_delta = jnp.einsum(
        "bck,bkm->bcm", covariance, incr_rows, preferred_element_type=jnp.float32
    )
    return correction_delta.astype(jnp.bfloat16)


def per_device(
    member_vectors,
    flow_speed_ratio,
    obs_pert,
    obs_incr,
    edge_list,
    block_obs,
    block_count,
    obs_offset,
):
    concentration_map = member_vectors
    outgoing = jnp.concatenate([concentration_map[-STEPS:, :], flow_speed_ratio[-STEPS:, None]], 1)
    arrived = passed_along(outgoing, "reg", 1)
    width = concentration_map.shape[1]
    halo = halo_rows(arrived[:, :-1], arrived[:, -1], width)
    concentration_map, first_guess_state = advect(halo, flow_speed_ratio, concentration_map)
    lend = edge_list.shape[2]
    edge_rows = edge_list.reshape(-1)
    own = obs_pert.shape[0]
    lent = (edge_rows[:, None] == jnp.arange(own)[None, :]).astype(jnp.bfloat16)
    chosen = jnp.stack(
        [
            jnp.dot(lent, obs_pert, preferred_element_type=jnp.float32).astype(jnp.bfloat16),
            jnp.dot(lent, obs_incr, preferred_element_type=jnp.float32).astype(jnp.bfloat16),
        ]
    )
    rimmed = padded(chosen, (("reg", 1),), lend)
    extended = jnp.concatenate(
        [rimmed[:, :lend], jnp.stack([obs_pert, obs_incr]), rimmed[:, -lend:]], 1
    )
    member_dev = member_vectors.shape[1]
    members = member_dev * lax.axis_size(MEM)
    per_region = block_obs.shape[0]
    parts = lax.axis_size(MEM)
    pairs = per_region // 2
    share = pairs // parts
    slots = extended.shape[1]
    picks = (block_obs.reshape(-1)[:, None] == jnp.arange(slots)[None, :]).astype(jnp.bfloat16)
    obs_rows = jnp.dot(picks, extended[0], preferred_element_type=jnp.float32).astype(jnp.bfloat16)
    incr_rows = jnp.dot(picks, extended[1], preferred_element_type=jnp.float32).astype(jnp.bfloat16)
    cells_p = first_guess_state.reshape(pairs, 2 * BLOCK, member_dev)
    obs_p = obs_rows.reshape(pairs, 2 * KB, member_dev)
    full = jnp.einsum("brm,blm->brl", cells_p, obs_p, preferred_element_type=jnp.float32)
    upper = (jnp.arange(2 * KB) >= KB)[None, None, :]
    cross = jnp.where(upper, full[:, BLOCK:, :], full[:, :BLOCK, :])
    sum_cells = jnp.sum(first_guess_state.astype(jnp.float32), 1).reshape(pairs, 1, 2 * BLOCK)
    sum_obs = jnp.sum(obs_rows.astype(jnp.float32), 1).reshape(pairs, 1, 2 * KB)
    payload = jnp.concatenate([cross, sum_cells, sum_obs], 1)
    got = lax.psum_scatter(
        payload.reshape(parts, share, BLOCK + 2, 2 * KB), MEM, scatter_dimension=0, tiled=True
    ).reshape(share, BLOCK + 2, 2 * KB)
    cross = got[:, :BLOCK, :]
    cells_sum = jnp.transpose(got[:, BLOCK, :].reshape(share, 2, BLOCK), (0, 2, 1))
    cells_sum = jnp.broadcast_to(cells_sum[:, :, :, None], (share, BLOCK, 2, KB)).reshape(
        share, BLOCK, 2 * KB
    )
    obs_sum = got[:, BLOCK + 1, :][:, None, :]
    first_block = lax.axis_index(MEM) * share * 2
    live_counts = lax.dynamic_slice_in_dim(block_count, first_block, share * 2, 0)
    positions = lax.dynamic_slice_in_dim(obs_offset, first_block, share * 2, 0)
    position = jnp.arange(BLOCK).astype(jnp.float32)
    distance = (position[None, :, None] - positions.reshape(share, 1, 2 * KB)) / (0.5 * BLOCK)
    lane = jnp.arange(2 * KB)
    counts = live_counts.reshape(share, 2)[:, lane // KB]
    active = (lane % KB)[None, :] < counts
    taper = jnp.where(active[:, None, :], 1.0 / (1.0 + distance * distance), 0.0)
    own_cov = (
        (cross - cells_sum * obs_sum / members) / (members - 1) * taper
    ).astype(jnp.bfloat16)
    covariance = gathered_copies(own_cov, MEM, 0)
    same_block = (jnp.arange(2 * BLOCK) // BLOCK)[:, None] == (lane // KB)[None, :]
    spread = jnp.where(same_block[None], jnp.concatenate([covariance, covariance], 1), 0)
    incr_p = incr_rows.reshape(pairs, 2 * KB, member_dev)
    correction_delta = jnp.einsum(
        "brl,blm->brm", spread, incr_p, preferred_element_type=jnp.float32
    ).astype(jnp.bfloat16)
    returned = correction_delta.reshape(per_region * BLOCK, member_dev)
    return concentration_map + returned.astype(jnp.float32)


def solution(mesh):
    mem, reg = mesh.devices.shape
    split = Mesh(mesh.devices.reshape(mem // CORES, CORES, reg), ("z", "core", "reg"))
    return jax.shard_map(
        per_device,
        mesh=split,
        in_specs=(
            P("reg", MEM),
            P("reg"),
            P("reg", MEM),
            P("reg", MEM),
            P("reg", None, None),
            P("reg", None),
            P("reg"),
            P("reg", None),
        ),
        out_specs=P("reg", MEM),
        check_vma=False,
    )
```

```python
import jax
import jax.numpy as jnp
from jax import lax
from jax.experimental import pallas as pl
from jax.experimental.pallas import tpu as pltpu
from jax.sharding import Mesh, PartitionSpec as P

BLOCK = 64
KB = 64
STEPS = 4
ROWS = 4096
CORES = 2
MEM = ("z", "core")

def advect_kernel(halo_ref, s_ref, x_ref, f_ref, fb_ref, carry_ref):
    @pl.when(pl.program_id(0) == 0)
    def _():
        carry_ref[...] = halo_ref[...]
    x = x_ref[...]
    lanes = x.shape[1]
    s = jnp.concatenate(
        [jnp.broadcast_to(s_ref[q : q + 1, :], (lanes, lanes)).T for q in range(s_ref.shape[0])], 0
    )
    first = lax.broadcasted_iota(jnp.int32, x.shape, 0) == 0
    last = x.shape[0] - 1
    for k in range(STEPS):
        before = jnp.where(first, carry_ref[k : k + 1, :], pltpu.roll(x, 1, 0))
        carry_ref[k : k + 1, :] = x[last:, :]
        x = x - s * (x - before)
    f_ref[...] = x
    fb_ref[...] = x.astype(jnp.bfloat16)

def advect(halo, speeds, x, interpret=False):
    cells, width = x.shape
    rows = min(ROWS, cells)
    return pl.pallas_call(
        advect_kernel,
        grid=(cells // rows,),
        in_specs=[
            pl.BlockSpec((8, width), lambda t: (0, 0)),
            pl.BlockSpec((rows // width, width), lambda t: (t, 0)),
            pl.BlockSpec((rows, width), lambda t: (t, 0)),
        ],
        out_specs=[pl.BlockSpec((rows, width), lambda t: (t, 0)), pl.BlockSpec((rows, width), lambda t: (t, 0))],
        out_shape=[jax.ShapeDtypeStruct(x.shape, jnp.float32), jax.ShapeDtypeStruct(x.shape, jnp.bfloat16)],
        scratch_shapes=[pltpu.VMEM((8, width), jnp.float32)],
        compiler_params=pltpu.CompilerParams(dimension_semantics=("arbitrary",)),
        interpret=interpret,
    )(halo, speeds.reshape(-1, width), x)

def halo_rows(arrived, arrived_speeds, width):
    v = arrived
    rows = [v[-1]]
    for k in range(1, STEPS):
        v = v[1:] - arrived_speeds[k:, None] * (v[1:] - v[:-1])
        rows.append(v[-1])
    return jnp.concatenate([jnp.stack(rows), jnp.zeros((8 - STEPS, width), v.dtype)], 0)


def passed_along(block, axis, distance):
    devices = range(lax.axis_size(axis))
    route = [((i - distance) % len(devices), i) for i in devices]
    return lax.ppermute(block, axis, route)


def padded(block, sides, width):
    for axis, dim in sides:
        count = lax.axis_size(axis)
        forward = [(i, i + 1) for i in range(count - 1)]
        forward.append((count - 1, 0))
        backward = [(target, source) for source, target in forward]
        low = lax.ppermute(
            lax.slice_in_dim(block, block.shape[dim] - width, None, axis=dim), axis, forward
        )
        high = lax.ppermute(lax.slice_in_dim(block, 0, width, axis=dim), axis, backward)
        block = jnp.concatenate([low, block, high], axis=dim)
    return block


def side_by_side(arrays, axis, dim, along):
    columns = [a.reshape(*a.shape[:along], -1) for a in arrays]
    both = jnp.concatenate(columns, axis=along)
    whole, at, gathered = (lax.psum_scatter(both, axis, scatter_dimension=dim, tiled=True), 0, [])
    for a, column in zip(arrays, columns):
        piece = whole[..., at : at + column.shape[along]]
        gathered.append(piece.reshape(*piece.shape[:along], *a.shape[along:]))
        at += column.shape[along]
    return tuple(gathered)


def laid_out(parts, dim):
    parts = jnp.moveaxis(parts, 0, dim)
    lengths = parts.shape
    return parts.reshape(*lengths[:dim], lengths[dim] * lengths[dim + 1], *lengths[dim + 2 :])


def from_everyone(value, axis):
    copies = jnp.broadcast_to(value, (lax.axis_size(axis), *value.shape))
    return lax.all_to_all(copies, axis, split_axis=0, concat_axis=0, tiled=True)


def gathered_copies(value, axis, dim):
    chips, cores = lax.axis_size("z"), lax.axis_size("core")
    along_z = lax.all_to_all(
        jnp.broadcast_to(value, (chips, *value.shape)), "z", split_axis=0, concat_axis=0, tiled=True
    )
    both = lax.all_to_all(
        jnp.broadcast_to(along_z, (cores, *along_z.shape)), "core", split_axis=0, concat_axis=0, tiled=True
    )
    return laid_out(jnp.swapaxes(both, 0, 1).reshape(chips * cores, *value.shape), dim)


def taper_mask(positions, live_counts):
    position = jnp.arange(BLOCK).astype(jnp.float32)
    distance = (position[None, :, None] - positions[:, None, :]) / (0.5 * BLOCK)
    active = jnp.arange(KB)[None, :] < live_counts[:, None]
    return jnp.where(active[:, None, :], 1.0 / (1.0 + distance * distance), 0.0)


def block_sums(mesh_point_entries, obs_rows):
    cross = jnp.einsum(
        "bcm,bkm->bck", mesh_point_entries, obs_rows, preferred_element_type=jnp.float32
    )
    sum_cells = jnp.sum(mesh_point_entries.astype(jnp.float32), 2)
    sum_obs = jnp.sum(obs_rows.astype(jnp.float32), 2)
    return (cross, sum_cells, sum_obs)


def covariances(cross, sum_cells, sum_obs, positions, live_counts, members):
    return (
        (cross - sum_cells[:, :, None] * sum_obs[:, None, :] / members)
        / (members - 1)
        * taper_mask(positions, live_counts)
    ).astype(jnp.bfloat16)


def apply_cov(covariance, incr_rows):
    correction_delta = jnp.einsum(
        "bck,bkm->bcm", covariance, incr_rows, preferred_element_type=jnp.float32
    )
    return correction_delta.astype(jnp.bfloat16)


def per_device(
    member_vectors,
    flow_speed_ratio,
    obs_pert,
    obs_incr,
    edge_list,
    block_obs,
    block_count,
    obs_offset,
):
    concentration_map = member_vectors
    outgoing = jnp.concatenate([concentration_map[-STEPS:, :], flow_speed_ratio[-STEPS:, None]], 1)
    arrived = passed_along(outgoing, "reg", 1)
    width = concentration_map.shape[1]
    halo = halo_rows(arrived[:, :-1], arrived[:, -1], width)
    concentration_map, first_guess_state = advect(halo, flow_speed_ratio, concentration_map)
    lend = edge_list.shape[2]
    edge_rows = edge_list.reshape(-1)
    own = obs_pert.shape[0]
    lent = (edge_rows[:, None] == jnp.arange(own)[None, :]).astype(jnp.bfloat16)
    chosen = jnp.stack(
        [
            jnp.dot(lent, obs_pert, preferred_element_type=jnp.float32).astype(jnp.bfloat16),
            jnp.dot(lent, obs_incr, preferred_element_type=jnp.float32).astype(jnp.bfloat16),
        ]
    )
    rimmed = padded(chosen, (("reg", 1),), lend)
    extended = jnp.concatenate(
        [rimmed[:, :lend], jnp.stack([obs_pert, obs_incr]), rimmed[:, -lend:]], 1
    )
    member_dev = member_vectors.shape[1]
    members = member_dev * lax.axis_size(MEM)
    per_region = block_obs.shape[0]
    parts = lax.axis_size(MEM)
    pairs = per_region // 2
    share = pairs // parts
    slots = extended.shape[1]
    picks = (block_obs.reshape(-1)[:, None] == jnp.arange(slots)[None, :]).astype(jnp.bfloat16)
    obs_rows = jnp.dot(picks, extended[0], preferred_element_type=jnp.float32).astype(jnp.bfloat16)
    incr_rows = jnp.dot(picks, extended[1], preferred_element_type=jnp.float32).astype(jnp.bfloat16)
    cells_p = first_guess_state.reshape(pairs, 2 * BLOCK, member_dev)
    obs_p = obs_rows.reshape(pairs, 2 * KB, member_dev)
    full = jnp.einsum("brm,blm->brl", cells_p, obs_p, preferred_element_type=jnp.float32)
    upper = (jnp.arange(2 * KB) >= KB)[None, None, :]
    cross = jnp.where(upper, full[:, BLOCK:, :], full[:, :BLOCK, :])
    sum_cells = jnp.sum(first_guess_state.astype(jnp.float32), 1).reshape(pairs, 1, 2 * BLOCK)
    sum_obs = jnp.sum(obs_rows.astype(jnp.float32), 1).reshape(pairs, 1, 2 * KB)
    payload = jnp.concatenate([cross, sum_cells, sum_obs], 1)
    got = lax.psum_scatter(
        payload.reshape(parts, share, BLOCK + 2, 2 * KB), MEM, scatter_dimension=0, tiled=True
    ).reshape(share, BLOCK + 2, 2 * KB)
    cross = got[:, :BLOCK, :]
    cells_sum = jnp.transpose(got[:, BLOCK, :].reshape(share, 2, BLOCK), (0, 2, 1))
    cells_sum = jnp.broadcast_to(cells_sum[:, :, :, None], (share, BLOCK, 2, KB)).reshape(
        share, BLOCK, 2 * KB
    )
    obs_sum = got[:, BLOCK + 1, :][:, None, :]
    first_block = lax.axis_index(MEM) * share * 2
    live_counts = lax.dynamic_slice_in_dim(block_count, first_block, share * 2, 0)
    positions = lax.dynamic_slice_in_dim(obs_offset, first_block, share * 2, 0)
    position = jnp.arange(BLOCK).astype(jnp.float32)
    distance = (position[None, :, None] - positions.reshape(share, 1, 2 * KB)) / (0.5 * BLOCK)
    lane = jnp.arange(2 * KB)
    counts = live_counts.reshape(share, 2)[:, lane // KB]
    active = (lane % KB)[None, :] < counts
    taper = jnp.where(active[:, None, :], 1.0 / (1.0 + distance * distance), 0.0)
    own_cov = (
        (cross - cells_sum * obs_sum / members) / (members - 1) * taper
    ).astype(jnp.bfloat16)
    covariance = gathered_copies(own_cov, MEM, 0)
    same_block = (jnp.arange(2 * BLOCK) // BLOCK)[:, None] == (lane // KB)[None, :]
    spread = jnp.where(same_block[None], jnp.concatenate([covariance, covariance], 1), 0)
    incr_p = incr_rows.reshape(pairs, 2 * KB, member_dev)
    correction_delta = jnp.einsum(
        "brl,blm->brm", spread, incr_p, preferred_element_type=jnp.float32
    ).astype(jnp.bfloat16)
    returned = correction_delta.reshape(per_region * BLOCK, member_dev)
    return concentration_map + returned.astype(jnp.float32)


def solution(mesh):
    mem, reg = mesh.devices.shape
    split = Mesh(mesh.devices.reshape(mem // CORES, CORES, reg), ("z", "core", "reg"))
    return jax.shard_map(
        per_device,
        mesh=split,
        in_specs=(
            P("reg", MEM),
            P("reg"),
            P("reg", MEM),
            P("reg", MEM),
            P("reg", None, None),
            P("reg", None),
            P("reg"),
            P("reg", None),
        ),
        out_specs=P("reg", MEM),
        check_vma=False,
    )
```

```python
import jax
import jax.numpy as jnp
from jax import lax
from jax.experimental import pallas as pl
from jax.experimental.pallas import tpu as pltpu
from jax.sharding import Mesh, PartitionSpec as P

BLOCK = 64
KB = 64
STEPS = 4
ROWS = 4096
CORES = 2
MEM = ("z", "core")

def advect_kernel(halo_ref, s_ref, x_ref, f_ref, fb_ref, sum_ref, carry_ref):
    @pl.when(pl.program_id(0) == 0)
    def _():
        carry_ref[...] = halo_ref[...]
    x = x_ref[...]
    lanes = x.shape[1]
    s = jnp.concatenate(
        [jnp.broadcast_to(s_ref[q : q + 1, :], (lanes, lanes)).T for q in range(s_ref.shape[0])], 0
    )
    first = lax.broadcasted_iota(jnp.int32, x.shape, 0) == 0
    last = x.shape[0] - 1
    for k in range(STEPS):
        before = jnp.where(first, carry_ref[k : k + 1, :], pltpu.roll(x, 1, 0))
        carry_ref[k : k + 1, :] = x[last:, :]
        x = x - s * (x - before)
    f_ref[...] = x
    rounded = x.astype(jnp.bfloat16)
    fb_ref[...] = rounded
    totals = jnp.sum(rounded.astype(jnp.float32), axis=1, keepdims=True)
    for q in range(sum_ref.shape[0]):
        column = jnp.broadcast_to(totals[q * lanes : (q + 1) * lanes, :], (lanes, lanes))
        sum_ref[q : q + 1, :] = column.T[0:1, :]

def advect(halo, speeds, x, interpret=False):
    cells, width = x.shape
    rows = min(ROWS, cells)
    return pl.pallas_call(
        advect_kernel,
        grid=(cells // rows,),
        in_specs=[
            pl.BlockSpec((8, width), lambda t: (0, 0)),
            pl.BlockSpec((rows // width, width), lambda t: (t, 0)),
            pl.BlockSpec((rows, width), lambda t: (t, 0)),
        ],
        out_specs=[
            pl.BlockSpec((rows, width), lambda t: (t, 0)),
            pl.BlockSpec((rows, width), lambda t: (t, 0)),
            pl.BlockSpec((rows // width, width), lambda t: (t, 0)),
        ],
        out_shape=[
            jax.ShapeDtypeStruct(x.shape, jnp.float32),
            jax.ShapeDtypeStruct(x.shape, jnp.bfloat16),
            jax.ShapeDtypeStruct((cells // width, width), jnp.float32),
        ],
        scratch_shapes=[pltpu.VMEM((8, width), jnp.float32)],
        compiler_params=pltpu.CompilerParams(dimension_semantics=("arbitrary",)),
        interpret=interpret,
    )(halo, speeds.reshape(-1, width), x)

def halo_rows(arrived, arrived_speeds, width):
    v = arrived
    rows = [v[-1]]
    for k in range(1, STEPS):
        v = v[1:] - arrived_speeds[k:, None] * (v[1:] - v[:-1])
        rows.append(v[-1])
    return jnp.concatenate([jnp.stack(rows), jnp.zeros((8 - STEPS, width), v.dtype)], 0)


def passed_along(block, axis, distance):
    devices = range(lax.axis_size(axis))
    route = [((i - distance) % len(devices), i) for i in devices]
    return lax.ppermute(block, axis, route)


def padded(block, sides, width):
    for axis, dim in sides:
        count = lax.axis_size(axis)
        forward = [(i, i + 1) for i in range(count - 1)]
        forward.append((count - 1, 0))
        backward = [(target, source) for source, target in forward]
        low = lax.ppermute(
            lax.slice_in_dim(block, block.shape[dim] - width, None, axis=dim), axis, forward
        )
        high = lax.ppermute(lax.slice_in_dim(block, 0, width, axis=dim), axis, backward)
        block = jnp.concatenate([low, block, high], axis=dim)
    return block


def side_by_side(arrays, axis, dim, along):
    columns = [a.reshape(*a.shape[:along], -1) for a in arrays]
    both = jnp.concatenate(columns, axis=along)
    whole, at, gathered = (lax.psum_scatter(both, axis, scatter_dimension=dim, tiled=True), 0, [])
    for a, column in zip(arrays, columns):
        piece = whole[..., at : at + column.shape[along]]
        gathered.append(piece.reshape(*piece.shape[:along], *a.shape[along:]))
        at += column.shape[along]
    return tuple(gathered)


def laid_out(parts, dim):
    parts = jnp.moveaxis(parts, 0, dim)
    lengths = parts.shape
    return parts.reshape(*lengths[:dim], lengths[dim] * lengths[dim + 1], *lengths[dim + 2 :])


def from_everyone(value, axis):
    copies = jnp.broadcast_to(value, (lax.axis_size(axis), *value.shape))
    return lax.all_to_all(copies, axis, split_axis=0, concat_axis=0, tiled=True)


def gathered_copies(value, axis, dim):
    chips, cores = lax.axis_size("z"), lax.axis_size("core")
    along_z = lax.all_to_all(
        jnp.broadcast_to(value, (chips, *value.shape)), "z", split_axis=0, concat_axis=0, tiled=True
    )
    both = lax.all_to_all(
        jnp.broadcast_to(along_z, (cores, *along_z.shape)), "core", split_axis=0, concat_axis=0, tiled=True
    )
    return laid_out(jnp.swapaxes(both, 0, 1).reshape(chips * cores, *value.shape), dim)


def taper_mask(positions, live_counts):
    position = jnp.arange(BLOCK).astype(jnp.float32)
    distance = (position[None, :, None] - positions[:, None, :]) / (0.5 * BLOCK)
    active = jnp.arange(KB)[None, :] < live_counts[:, None]
    return jnp.where(active[:, None, :], 1.0 / (1.0 + distance * distance), 0.0)


def block_sums(mesh_point_entries, obs_rows):
    cross = jnp.einsum(
        "bcm,bkm->bck", mesh_point_entries, obs_rows, preferred_element_type=jnp.float32
    )
    sum_cells = jnp.sum(mesh_point_entries.astype(jnp.float32), 2)
    sum_obs = jnp.sum(obs_rows.astype(jnp.float32), 2)
    return (cross, sum_cells, sum_obs)


def covariances(cross, sum_cells, sum_obs, positions, live_counts, members):
    return (
        (cross - sum_cells[:, :, None] * sum_obs[:, None, :] / members)
        / (members - 1)
        * taper_mask(positions, live_counts)
    ).astype(jnp.bfloat16)


def apply_cov(covariance, incr_rows):
    correction_delta = jnp.einsum(
        "bck,bkm->bcm", covariance, incr_rows, preferred_element_type=jnp.float32
    )
    return correction_delta.astype(jnp.bfloat16)


def per_device(
    member_vectors,
    flow_speed_ratio,
    obs_pert,
    obs_incr,
    edge_list,
    block_obs,
    block_count,
    obs_offset,
):
    concentration_map = member_vectors
    outgoing = jnp.concatenate([concentration_map[-STEPS:, :], flow_speed_ratio[-STEPS:, None]], 1)
    arrived = passed_along(outgoing, "reg", 1)
    width = concentration_map.shape[1]
    halo = halo_rows(arrived[:, :-1], arrived[:, -1], width)
    concentration_map, first_guess_state, cell_sums = advect(halo, flow_speed_ratio, concentration_map)
    lend = edge_list.shape[2]
    edge_rows = edge_list.reshape(-1)
    own = obs_pert.shape[0]
    lent = (edge_rows[:, None] == jnp.arange(own)[None, :]).astype(jnp.bfloat16)
    chosen = jnp.stack(
        [
            jnp.dot(lent, obs_pert, preferred_element_type=jnp.float32).astype(jnp.bfloat16),
            jnp.dot(lent, obs_incr, preferred_element_type=jnp.float32).astype(jnp.bfloat16),
        ]
    )
    rimmed = padded(chosen, (("reg", 1),), lend)
    extended = jnp.concatenate(
        [rimmed[:, :lend], jnp.stack([obs_pert, obs_incr]), rimmed[:, -lend:]], 1
    )
    member_dev = member_vectors.shape[1]
    members = member_dev * lax.axis_size(MEM)
    per_region = block_obs.shape[0]
    parts = lax.axis_size(MEM)
    pairs = per_region // 2
    share = pairs // parts
    slots = extended.shape[1]
    picks = (block_obs.reshape(-1)[:, None] == jnp.arange(slots)[None, :]).astype(jnp.bfloat16)
    obs_rows = jnp.dot(picks, extended[0], preferred_element_type=jnp.float32).astype(jnp.bfloat16)
    incr_rows = jnp.dot(picks, extended[1], preferred_element_type=jnp.float32).astype(jnp.bfloat16)
    cells_p = first_guess_state.reshape(pairs, 2 * BLOCK, member_dev)
    obs_p = obs_rows.reshape(pairs, 2 * KB, member_dev)
    full = jnp.einsum("brm,blm->brl", cells_p, obs_p, preferred_element_type=jnp.float32)
    upper = (jnp.arange(2 * KB) >= KB)[None, None, :]
    cross = jnp.where(upper, full[:, BLOCK:, :], full[:, :BLOCK, :])
    sum_cells = cell_sums.reshape(pairs, 1, 2 * BLOCK)
    sum_obs = jnp.sum(obs_rows.astype(jnp.float32), 1).reshape(pairs, 1, 2 * KB)
    payload = jnp.concatenate([cross, sum_cells, sum_obs], 1)
    got = lax.psum_scatter(
        payload.reshape(parts, share, BLOCK + 2, 2 * KB), MEM, scatter_dimension=0, tiled=True
    ).reshape(share, BLOCK + 2, 2 * KB)
    cross = got[:, :BLOCK, :]
    cells_sum = jnp.transpose(got[:, BLOCK, :].reshape(share, 2, BLOCK), (0, 2, 1))
    cells_sum = jnp.broadcast_to(cells_sum[:, :, :, None], (share, BLOCK, 2, KB)).reshape(
        share, BLOCK, 2 * KB
    )
    obs_sum = got[:, BLOCK + 1, :][:, None, :]
    first_block = lax.axis_index(MEM) * share * 2
    live_counts = lax.dynamic_slice_in_dim(block_count, first_block, share * 2, 0)
    positions = lax.dynamic_slice_in_dim(obs_offset, first_block, share * 2, 0)
    position = jnp.arange(BLOCK).astype(jnp.float32)
    distance = (position[None, :, None] - positions.reshape(share, 1, 2 * KB)) / (0.5 * BLOCK)
    lane = jnp.arange(2 * KB)
    counts = live_counts.reshape(share, 2)[:, lane // KB]
    active = (lane % KB)[None, :] < counts
    taper = jnp.where(active[:, None, :], 1.0 / (1.0 + distance * distance), 0.0)
    own_cov = (
        (cross - cells_sum * obs_sum / members) / (members - 1) * taper
    ).astype(jnp.bfloat16)
    covariance = gathered_copies(own_cov, MEM, 0)
    same_block = (jnp.arange(2 * BLOCK) // BLOCK)[:, None] == (lane // KB)[None, :]
    spread = jnp.where(same_block[None], jnp.concatenate([covariance, covariance], 1), 0)
    incr_p = incr_rows.reshape(pairs, 2 * KB, member_dev)
    correction_delta = jnp.einsum(
        "brl,blm->brm", spread, incr_p, preferred_element_type=jnp.float32
    ).astype(jnp.bfloat16)
    returned = correction_delta.reshape(per_region * BLOCK, member_dev)
    return concentration_map + returned.astype(jnp.float32)


def solution(mesh):
    mem, reg = mesh.devices.shape
    split = Mesh(mesh.devices.reshape(mem // CORES, CORES, reg), ("z", "core", "reg"))
    return jax.shard_map(
        per_device,
        mesh=split,
        in_specs=(
            P("reg", MEM),
            P("reg"),
            P("reg", MEM),
            P("reg", MEM),
            P("reg", None, None),
            P("reg", None),
            P("reg"),
            P("reg", None),
        ),
        out_specs=P("reg", MEM),
        check_vma=False,
    )
```

```python
import jax
import jax.numpy as jnp
from jax import lax
from jax.experimental import pallas as pl
from jax.experimental.pallas import tpu as pltpu
from jax.sharding import Mesh, PartitionSpec as P

BLOCK = 64
KB = 64
STEPS = 4
ROWS = 4096
CORES = 2
MEM = ("z", "core")

def advect_kernel(halo_ref, s_ref, x_ref, f_ref, fb_ref, sum_ref, carry_ref):
    @pl.when(pl.program_id(0) == 0)
    def _():
        carry_ref[...] = halo_ref[...]
    x = x_ref[...]
    lanes = x.shape[1]
    s = jnp.concatenate(
        [jnp.broadcast_to(s_ref[q : q + 1, :], (lanes, lanes)).T for q in range(s_ref.shape[0])], 0
    )
    first = lax.broadcasted_iota(jnp.int32, x.shape, 0) == 0
    last = x.shape[0] - 1
    for k in range(STEPS):
        before = jnp.where(first, carry_ref[k : k + 1, :], pltpu.roll(x, 1, 0))
        carry_ref[k : k + 1, :] = x[last:, :]
        x = x - s * (x - before)
    f_ref[...] = x
    rounded = x.astype(jnp.bfloat16)
    fb_ref[...] = rounded
    totals = jnp.sum(rounded.astype(jnp.float32), axis=1, keepdims=True)
    for q in range(sum_ref.shape[0]):
        column = jnp.broadcast_to(totals[q * lanes : (q + 1) * lanes, :], (lanes, lanes))
        sum_ref[q : q + 1, :] = column.T[0:1, :]

def advect(halo, speeds, x, interpret=False):
    cells, width = x.shape
    rows = min(ROWS, cells)
    return pl.pallas_call(
        advect_kernel,
        grid=(cells // rows,),
        in_specs=[
            pl.BlockSpec((8, width), lambda t: (0, 0)),
            pl.BlockSpec((rows // width, width), lambda t: (t, 0)),
            pl.BlockSpec((rows, width), lambda t: (t, 0)),
        ],
        out_specs=[
            pl.BlockSpec((rows, width), lambda t: (t, 0)),
            pl.BlockSpec((rows, width), lambda t: (t, 0)),
            pl.BlockSpec((rows // width, width), lambda t: (t, 0)),
        ],
        out_shape=[
            jax.ShapeDtypeStruct(x.shape, jnp.float32),
            jax.ShapeDtypeStruct(x.shape, jnp.bfloat16),
            jax.ShapeDtypeStruct((cells // width, width), jnp.float32),
        ],
        scratch_shapes=[pltpu.VMEM((8, width), jnp.float32)],
        compiler_params=pltpu.CompilerParams(dimension_semantics=("arbitrary",)),
        interpret=interpret,
    )(halo, speeds.reshape(-1, width), x)

def halo_rows(arrived, arrived_speeds, width):
    v = arrived
    rows = [v[-1]]
    for k in range(1, STEPS):
        v = v[1:] - arrived_speeds[k:, None] * (v[1:] - v[:-1])
        rows.append(v[-1])
    return jnp.concatenate([jnp.stack(rows), jnp.zeros((8 - STEPS, width), v.dtype)], 0)


def passed_along(block, axis, distance):
    devices = range(lax.axis_size(axis))
    route = [((i - distance) % len(devices), i) for i in devices]
    return lax.ppermute(block, axis, route)


def padded(block, sides, width):
    for axis, dim in sides:
        count = lax.axis_size(axis)
        forward = [(i, i + 1) for i in range(count - 1)]
        forward.append((count - 1, 0))
        backward = [(target, source) for source, target in forward]
        low = lax.ppermute(
            lax.slice_in_dim(block, block.shape[dim] - width, None, axis=dim), axis, forward
        )
        high = lax.ppermute(lax.slice_in_dim(block, 0, width, axis=dim), axis, backward)
        block = jnp.concatenate([low, block, high], axis=dim)
    return block


def side_by_side(arrays, axis, dim, along):
    columns = [a.reshape(*a.shape[:along], -1) for a in arrays]
    both = jnp.concatenate(columns, axis=along)
    whole, at, gathered = (lax.psum_scatter(both, axis, scatter_dimension=dim, tiled=True), 0, [])
    for a, column in zip(arrays, columns):
        piece = whole[..., at : at + column.shape[along]]
        gathered.append(piece.reshape(*piece.shape[:along], *a.shape[along:]))
        at += column.shape[along]
    return tuple(gathered)


def laid_out(parts, dim):
    parts = jnp.moveaxis(parts, 0, dim)
    lengths = parts.shape
    return parts.reshape(*lengths[:dim], lengths[dim] * lengths[dim + 1], *lengths[dim + 2 :])


def from_everyone(value, axis):
    copies = jnp.broadcast_to(value, (lax.axis_size(axis), *value.shape))
    return lax.all_to_all(copies, axis, split_axis=0, concat_axis=0, tiled=True)


def gathered_copies(value, axis, dim):
    chips, cores = lax.axis_size("z"), lax.axis_size("core")
    along_z = lax.all_to_all(
        jnp.broadcast_to(value, (chips, *value.shape)), "z", split_axis=0, concat_axis=0, tiled=True
    )
    other = lax.ppermute(along_z, "core", [(0, 1), (1, 0)])
    low = lax.axis_index("core") == 0
    both = jnp.stack([jnp.where(low, along_z, other), jnp.where(low, other, along_z)])
    return laid_out(jnp.swapaxes(both, 0, 1).reshape(chips * cores, *value.shape), dim)


def taper_mask(positions, live_counts):
    position = jnp.arange(BLOCK).astype(jnp.float32)
    distance = (position[None, :, None] - positions[:, None, :]) / (0.5 * BLOCK)
    active = jnp.arange(KB)[None, :] < live_counts[:, None]
    return jnp.where(active[:, None, :], 1.0 / (1.0 + distance * distance), 0.0)


def block_sums(mesh_point_entries, obs_rows):
    cross = jnp.einsum(
        "bcm,bkm->bck", mesh_point_entries, obs_rows, preferred_element_type=jnp.float32
    )
    sum_cells = jnp.sum(mesh_point_entries.astype(jnp.float32), 2)
    sum_obs = jnp.sum(obs_rows.astype(jnp.float32), 2)
    return (cross, sum_cells, sum_obs)


def covariances(cross, sum_cells, sum_obs, positions, live_counts, members):
    return (
        (cross - sum_cells[:, :, None] * sum_obs[:, None, :] / members)
        / (members - 1)
        * taper_mask(positions, live_counts)
    ).astype(jnp.bfloat16)


def apply_cov(covariance, incr_rows):
    correction_delta = jnp.einsum(
        "bck,bkm->bcm", covariance, incr_rows, preferred_element_type=jnp.float32
    )
    return correction_delta.astype(jnp.bfloat16)


def per_device(
    member_vectors,
    flow_speed_ratio,
    obs_pert,
    obs_incr,
    edge_list,
    block_obs,
    block_count,
    obs_offset,
):
    concentration_map = member_vectors
    outgoing = jnp.concatenate([concentration_map[-STEPS:, :], flow_speed_ratio[-STEPS:, None]], 1)
    arrived = passed_along(outgoing, "reg", 1)
    width = concentration_map.shape[1]
    halo = halo_rows(arrived[:, :-1], arrived[:, -1], width)
    concentration_map, first_guess_state, cell_sums = advect(halo, flow_speed_ratio, concentration_map)
    lend = edge_list.shape[2]
    edge_rows = edge_list.reshape(-1)
    own = obs_pert.shape[0]
    lent = (edge_rows[:, None] == jnp.arange(own)[None, :]).astype(jnp.bfloat16)
    chosen = jnp.stack(
        [
            jnp.dot(lent, obs_pert, preferred_element_type=jnp.float32).astype(jnp.bfloat16),
            jnp.dot(lent, obs_incr, preferred_element_type=jnp.float32).astype(jnp.bfloat16),
        ]
    )
    rimmed = padded(chosen, (("reg", 1),), lend)
    extended = jnp.concatenate(
        [rimmed[:, :lend], jnp.stack([obs_pert, obs_incr]), rimmed[:, -lend:]], 1
    )
    member_dev = member_vectors.shape[1]
    members = member_dev * lax.axis_size(MEM)
    per_region = block_obs.shape[0]
    parts = lax.axis_size(MEM)
    pairs = per_region // 2
    share = pairs // parts
    slots = extended.shape[1]
    picks = (block_obs.reshape(-1)[:, None] == jnp.arange(slots)[None, :]).astype(jnp.bfloat16)
    obs_rows = jnp.dot(picks, extended[0], preferred_element_type=jnp.float32).astype(jnp.bfloat16)
    incr_rows = jnp.dot(picks, extended[1], preferred_element_type=jnp.float32).astype(jnp.bfloat16)
    cells_p = first_guess_state.reshape(pairs, 2 * BLOCK, member_dev)
    obs_p = obs_rows.reshape(pairs, 2 * KB, member_dev)
    full = jnp.einsum("brm,blm->brl", cells_p, obs_p, preferred_element_type=jnp.float32)
    upper = (jnp.arange(2 * KB) >= KB)[None, None, :]
    cross = jnp.where(upper, full[:, BLOCK:, :], full[:, :BLOCK, :])
    sum_cells = cell_sums.reshape(pairs, 1, 2 * BLOCK)
    sum_obs = jnp.sum(obs_rows.astype(jnp.float32), 1).reshape(pairs, 1, 2 * KB)
    payload = jnp.concatenate([cross, sum_cells, sum_obs], 1)
    got = lax.psum_scatter(
        payload.reshape(parts, share, BLOCK + 2, 2 * KB), MEM, scatter_dimension=0, tiled=True
    ).reshape(share, BLOCK + 2, 2 * KB)
    cross = got[:, :BLOCK, :]
    cells_sum = jnp.transpose(got[:, BLOCK, :].reshape(share, 2, BLOCK), (0, 2, 1))
    cells_sum = jnp.broadcast_to(cells_sum[:, :, :, None], (share, BLOCK, 2, KB)).reshape(
        share, BLOCK, 2 * KB
    )
    obs_sum = got[:, BLOCK + 1, :][:, None, :]
    first_block = lax.axis_index(MEM) * share * 2
    live_counts = lax.dynamic_slice_in_dim(block_count, first_block, share * 2, 0)
    positions = lax.dynamic_slice_in_dim(obs_offset, first_block, share * 2, 0)
    position = jnp.arange(BLOCK).astype(jnp.float32)
    distance = (position[None, :, None] - positions.reshape(share, 1, 2 * KB)) / (0.5 * BLOCK)
    lane = jnp.arange(2 * KB)
    counts = live_counts.reshape(share, 2)[:, lane // KB]
    active = (lane % KB)[None, :] < counts
    taper = jnp.where(active[:, None, :], 1.0 / (1.0 + distance * distance), 0.0)
    own_cov = (
        (cross - cells_sum * obs_sum / members) / (members - 1) * taper
    ).astype(jnp.bfloat16)
    covariance = gathered_copies(own_cov, MEM, 0)
    same_block = (jnp.arange(2 * BLOCK) // BLOCK)[:, None] == (lane // KB)[None, :]
    spread = jnp.where(same_block[None], jnp.concatenate([covariance, covariance], 1), 0)
    incr_p = incr_rows.reshape(pairs, 2 * KB, member_dev)
    correction_delta = jnp.einsum(
        "brl,blm->brm", spread, incr_p, preferred_element_type=jnp.float32
    ).astype(jnp.bfloat16)
    returned = correction_delta.reshape(per_region * BLOCK, member_dev)
    return concentration_map + returned.astype(jnp.float32)


def solution(mesh):
    mem, reg = mesh.devices.shape
    split = Mesh(mesh.devices.reshape(mem // CORES, CORES, reg), ("z", "core", "reg"))
    return jax.shard_map(
        per_device,
        mesh=split,
        in_specs=(
            P("reg", MEM),
            P("reg"),
            P("reg", MEM),
            P("reg", MEM),
            P("reg", None, None),
            P("reg", None),
            P("reg"),
            P("reg", None),
        ),
        out_specs=P("reg", MEM),
        check_vma=False,
    )
```

```python
import jax
import jax.numpy as jnp
from jax import lax
from jax.experimental import pallas as pl
from jax.experimental.pallas import tpu as pltpu
from jax.sharding import Mesh, PartitionSpec as P

BLOCK = 64
KB = 64
STEPS = 4
ROWS = 4096
CORES = 2
MEM = ("z", "core")

def advect_kernel(halo_ref, s_ref, x_ref, f_ref, fb_ref, sum_ref, carry_ref):
    @pl.when(pl.program_id(0) == 0)
    def _():
        carry_ref[...] = halo_ref[...]
    x = x_ref[...]
    lanes = x.shape[1]
    s = jnp.concatenate(
        [jnp.broadcast_to(s_ref[q : q + 1, :], (lanes, lanes)).T for q in range(s_ref.shape[0])], 0
    )
    first = lax.broadcasted_iota(jnp.int32, x.shape, 0) == 0
    last = x.shape[0] - 1
    for k in range(STEPS):
        before = jnp.where(first, carry_ref[k : k + 1, :], pltpu.roll(x, 1, 0))
        carry_ref[k : k + 1, :] = x[last:, :]
        x = x - s * (x - before)
    f_ref[...] = x
    rounded = x.astype(jnp.bfloat16)
    fb_ref[...] = rounded
    totals = jnp.sum(rounded.astype(jnp.float32), axis=1, keepdims=True)
    for q in range(sum_ref.shape[0]):
        column = jnp.broadcast_to(totals[q * lanes : (q + 1) * lanes, :], (lanes, lanes))
        sum_ref[q : q + 1, :] = column.T[0:1, :]

def advect(halo, speeds, x, interpret=False):
    cells, width = x.shape
    rows = min(ROWS, cells)
    return pl.pallas_call(
        advect_kernel,
        grid=(cells // rows,),
        in_specs=[
            pl.BlockSpec((8, width), lambda t: (0, 0)),
            pl.BlockSpec((rows // width, width), lambda t: (t, 0)),
            pl.BlockSpec((rows, width), lambda t: (t, 0)),
        ],
        out_specs=[
            pl.BlockSpec((rows, width), lambda t: (t, 0)),
            pl.BlockSpec((rows, width), lambda t: (t, 0)),
            pl.BlockSpec((rows // width, width), lambda t: (t, 0)),
        ],
        out_shape=[
            jax.ShapeDtypeStruct(x.shape, jnp.float32),
            jax.ShapeDtypeStruct(x.shape, jnp.bfloat16),
            jax.ShapeDtypeStruct((cells // width, width), jnp.float32),
        ],
        scratch_shapes=[pltpu.VMEM((8, width), jnp.float32)],
        compiler_params=pltpu.CompilerParams(dimension_semantics=("arbitrary",)),
        interpret=interpret,
    )(halo, speeds.reshape(-1, width), x)

def halo_rows(arrived, arrived_speeds, width):
    v = arrived
    rows = [v[-1]]
    for k in range(1, STEPS):
        v = v[1:] - arrived_speeds[k:, None] * (v[1:] - v[:-1])
        rows.append(v[-1])
    return jnp.concatenate([jnp.stack(rows), jnp.zeros((8 - STEPS, width), v.dtype)], 0)


def passed_along(block, axis, distance):
    devices = range(lax.axis_size(axis))
    route = [((i - distance) % len(devices), i) for i in devices]
    return lax.ppermute(block, axis, route)


def padded(block, sides, width):
    for axis, dim in sides:
        count = lax.axis_size(axis)
        forward = [(i, i + 1) for i in range(count - 1)]
        forward.append((count - 1, 0))
        backward = [(target, source) for source, target in forward]
        low = lax.ppermute(
            lax.slice_in_dim(block, block.shape[dim] - width, None, axis=dim), axis, forward
        )
        high = lax.ppermute(lax.slice_in_dim(block, 0, width, axis=dim), axis, backward)
        block = jnp.concatenate([low, block, high], axis=dim)
    return block


def side_by_side(arrays, axis, dim, along):
    columns = [a.reshape(*a.shape[:along], -1) for a in arrays]
    both = jnp.concatenate(columns, axis=along)
    whole, at, gathered = (lax.psum_scatter(both, axis, scatter_dimension=dim, tiled=True), 0, [])
    for a, column in zip(arrays, columns):
        piece = whole[..., at : at + column.shape[along]]
        gathered.append(piece.reshape(*piece.shape[:along], *a.shape[along:]))
        at += column.shape[along]
    return tuple(gathered)


def laid_out(parts, dim):
    parts = jnp.moveaxis(parts, 0, dim)
    lengths = parts.shape
    return parts.reshape(*lengths[:dim], lengths[dim] * lengths[dim + 1], *lengths[dim + 2 :])


def from_everyone(value, axis):
    copies = jnp.broadcast_to(value, (lax.axis_size(axis), *value.shape))
    return lax.all_to_all(copies, axis, split_axis=0, concat_axis=0, tiled=True)


def gathered_copies(value, axis, dim):
    chips, cores = lax.axis_size("z"), lax.axis_size("core")
    along_z = lax.all_to_all(
        jnp.broadcast_to(value, (chips, *value.shape)), "z", split_axis=0, concat_axis=0, tiled=True
    )
    both = lax.all_to_all(
        jnp.broadcast_to(along_z, (cores, *along_z.shape)), "core", split_axis=0, concat_axis=0, tiled=True
    )
    return laid_out(jnp.swapaxes(both, 0, 1).reshape(chips * cores, *value.shape), dim)


def taper_mask(positions, live_counts):
    position = jnp.arange(BLOCK).astype(jnp.float32)
    distance = (position[None, :, None] - positions[:, None, :]) / (0.5 * BLOCK)
    active = jnp.arange(KB)[None, :] < live_counts[:, None]
    return jnp.where(active[:, None, :], 1.0 / (1.0 + distance * distance), 0.0)


def block_sums(mesh_point_entries, obs_rows):
    cross = jnp.einsum(
        "bcm,bkm->bck", mesh_point_entries, obs_rows, preferred_element_type=jnp.float32
    )
    sum_cells = jnp.sum(mesh_point_entries.astype(jnp.float32), 2)
    sum_obs = jnp.sum(obs_rows.astype(jnp.float32), 2)
    return (cross, sum_cells, sum_obs)


def covariances(cross, sum_cells, sum_obs, positions, live_counts, members):
    return (
        (cross - sum_cells[:, :, None] * sum_obs[:, None, :] / members)
        / (members - 1)
        * taper_mask(positions, live_counts)
    ).astype(jnp.bfloat16)


def apply_cov(covariance, incr_rows):
    correction_delta = jnp.einsum(
        "bck,bkm->bcm", covariance, incr_rows, preferred_element_type=jnp.float32
    )
    return correction_delta.astype(jnp.bfloat16)


def per_device(
    member_vectors,
    flow_speed_ratio,
    obs_pert,
    obs_incr,
    edge_list,
    block_obs,
    block_count,
    obs_offset,
):
    concentration_map = member_vectors
    outgoing = jnp.concatenate([concentration_map[-STEPS:, :], flow_speed_ratio[-STEPS:, None]], 1)
    arrived = passed_along(outgoing, "reg", 1)
    width = concentration_map.shape[1]
    halo = halo_rows(arrived[:, :-1], arrived[:, -1], width)
    concentration_map, first_guess_state, cell_sums = advect(halo, flow_speed_ratio, concentration_map)
    lend = edge_list.shape[2]
    edge_rows = edge_list.reshape(-1)
    own = obs_pert.shape[0]
    lent = (edge_rows[:, None] == jnp.arange(own)[None, :]).astype(jnp.bfloat16)
    member_dev = member_vectors.shape[1]
    lent_rows = jnp.dot(
        lent, jnp.concatenate([obs_pert, obs_incr], 1), preferred_element_type=jnp.float32
    ).astype(jnp.bfloat16)
    chosen = jnp.stack([lent_rows[:, :member_dev], lent_rows[:, member_dev:]])
    rimmed = padded(chosen, (("reg", 1),), lend)
    extended = jnp.concatenate(
        [rimmed[:, :lend], jnp.stack([obs_pert, obs_incr]), rimmed[:, -lend:]], 1
    )
    member_dev = member_vectors.shape[1]
    members = member_dev * lax.axis_size(MEM)
    per_region = block_obs.shape[0]
    parts = lax.axis_size(MEM)
    pairs = per_region // 2
    share = pairs // parts
    slots = extended.shape[1]
    picks = (block_obs.reshape(-1)[:, None] == jnp.arange(slots)[None, :]).astype(jnp.bfloat16)
    obs_rows = jnp.dot(picks, extended[0], preferred_element_type=jnp.float32).astype(jnp.bfloat16)
    incr_rows = jnp.dot(picks, extended[1], preferred_element_type=jnp.float32).astype(jnp.bfloat16)
    cells_p = first_guess_state.reshape(pairs, 2 * BLOCK, member_dev)
    obs_p = obs_rows.reshape(pairs, 2 * KB, member_dev)
    full = jnp.einsum("brm,blm->brl", cells_p, obs_p, preferred_element_type=jnp.float32)
    upper = (jnp.arange(2 * KB) >= KB)[None, None, :]
    cross = jnp.where(upper, full[:, BLOCK:, :], full[:, :BLOCK, :])
    sum_cells = cell_sums.reshape(pairs, 1, 2 * BLOCK)
    sum_obs = jnp.sum(obs_rows.astype(jnp.float32), 1).reshape(pairs, 1, 2 * KB)
    payload = jnp.concatenate([cross, sum_cells, sum_obs], 1)
    got = lax.psum_scatter(
        payload.reshape(parts, share, BLOCK + 2, 2 * KB), MEM, scatter_dimension=0, tiled=True
    ).reshape(share, BLOCK + 2, 2 * KB)
    cross = got[:, :BLOCK, :]
    cells_sum = jnp.transpose(got[:, BLOCK, :].reshape(share, 2, BLOCK), (0, 2, 1))
    cells_sum = jnp.broadcast_to(cells_sum[:, :, :, None], (share, BLOCK, 2, KB)).reshape(
        share, BLOCK, 2 * KB
    )
    obs_sum = got[:, BLOCK + 1, :][:, None, :]
    first_block = lax.axis_index(MEM) * share * 2
    live_counts = lax.dynamic_slice_in_dim(block_count, first_block, share * 2, 0)
    positions = lax.dynamic_slice_in_dim(obs_offset, first_block, share * 2, 0)
    position = jnp.arange(BLOCK).astype(jnp.float32)
    distance = (position[None, :, None] - positions.reshape(share, 1, 2 * KB)) / (0.5 * BLOCK)
    lane = jnp.arange(2 * KB)
    counts = live_counts.reshape(share, 2)[:, lane // KB]
    active = (lane % KB)[None, :] < counts
    taper = jnp.where(active[:, None, :], 1.0 / (1.0 + distance * distance), 0.0)
    own_cov = (
        (cross - cells_sum * obs_sum / members) / (members - 1) * taper
    ).astype(jnp.bfloat16)
    covariance = gathered_copies(own_cov, MEM, 0)
    same_block = (jnp.arange(2 * BLOCK) // BLOCK)[:, None] == (lane // KB)[None, :]
    spread = jnp.where(same_block[None], jnp.concatenate([covariance, covariance], 1), 0)
    incr_p = incr_rows.reshape(pairs, 2 * KB, member_dev)
    correction_delta = jnp.einsum(
        "brl,blm->brm", spread, incr_p, preferred_element_type=jnp.float32
    ).astype(jnp.bfloat16)
    returned = correction_delta.reshape(per_region * BLOCK, member_dev)
    return concentration_map + returned.astype(jnp.float32)


def solution(mesh):
    mem, reg = mesh.devices.shape
    split = Mesh(mesh.devices.reshape(mem // CORES, CORES, reg), ("z", "core", "reg"))
    return jax.shard_map(
        per_device,
        mesh=split,
        in_specs=(
            P("reg", MEM),
            P("reg"),
            P("reg", MEM),
            P("reg", MEM),
            P("reg", None, None),
            P("reg", None),
            P("reg"),
            P("reg", None),
        ),
        out_specs=P("reg", MEM),
        check_vma=False,
    )
```

```python
import jax
import jax.numpy as jnp
from jax import lax
from jax.experimental import pallas as pl
from jax.experimental.pallas import tpu as pltpu
from jax.sharding import Mesh, PartitionSpec as P

BLOCK = 64
KB = 64
STEPS = 4
ROWS = 8192
CORES = 2
MEM = ("z", "core")

def advect_kernel(halo_ref, s_ref, x_ref, f_ref, fb_ref, sum_ref, carry_ref):
    @pl.when(pl.program_id(0) == 0)
    def _():
        carry_ref[...] = halo_ref[...]
    x = x_ref[...]
    lanes = x.shape[1]
    s = jnp.concatenate(
        [jnp.broadcast_to(s_ref[q : q + 1, :], (lanes, lanes)).T for q in range(s_ref.shape[0])], 0
    )
    first = lax.broadcasted_iota(jnp.int32, x.shape, 0) == 0
    last = x.shape[0] - 1
    for k in range(STEPS):
        before = jnp.where(first, carry_ref[k : k + 1, :], pltpu.roll(x, 1, 0))
        carry_ref[k : k + 1, :] = x[last:, :]
        x = x - s * (x - before)
    f_ref[...] = x
    rounded = x.astype(jnp.bfloat16)
    fb_ref[...] = rounded
    totals = jnp.sum(rounded.astype(jnp.float32), axis=1, keepdims=True)
    for q in range(sum_ref.shape[0]):
        column = jnp.broadcast_to(totals[q * lanes : (q + 1) * lanes, :], (lanes, lanes))
        sum_ref[q : q + 1, :] = column.T[0:1, :]

def advect(halo, speeds, x, interpret=False):
    cells, width = x.shape
    rows = min(ROWS, cells)
    return pl.pallas_call(
        advect_kernel,
        grid=(cells // rows,),
        in_specs=[
            pl.BlockSpec((8, width), lambda t: (0, 0)),
            pl.BlockSpec((rows // width, width), lambda t: (t, 0)),
            pl.BlockSpec((rows, width), lambda t: (t, 0)),
        ],
        out_specs=[
            pl.BlockSpec((rows, width), lambda t: (t, 0)),
            pl.BlockSpec((rows, width), lambda t: (t, 0)),
            pl.BlockSpec((rows // width, width), lambda t: (t, 0)),
        ],
        out_shape=[
            jax.ShapeDtypeStruct(x.shape, jnp.float32),
            jax.ShapeDtypeStruct(x.shape, jnp.bfloat16),
            jax.ShapeDtypeStruct((cells // width, width), jnp.float32),
        ],
        scratch_shapes=[pltpu.VMEM((8, width), jnp.float32)],
        compiler_params=pltpu.CompilerParams(dimension_semantics=("arbitrary",)),
        interpret=interpret,
    )(halo, speeds.reshape(-1, width), x)

def halo_rows(arrived, arrived_speeds, width):
    v = arrived
    rows = [v[-1]]
    for k in range(1, STEPS):
        v = v[1:] - arrived_speeds[k:, None] * (v[1:] - v[:-1])
        rows.append(v[-1])
    return jnp.concatenate([jnp.stack(rows), jnp.zeros((8 - STEPS, width), v.dtype)], 0)


def passed_along(block, axis, distance):
    devices = range(lax.axis_size(axis))
    route = [((i - distance) % len(devices), i) for i in devices]
    return lax.ppermute(block, axis, route)


def padded(block, sides, width):
    for axis, dim in sides:
        count = lax.axis_size(axis)
        forward = [(i, i + 1) for i in range(count - 1)]
        forward.append((count - 1, 0))
        backward = [(target, source) for source, target in forward]
        low = lax.ppermute(
            lax.slice_in_dim(block, block.shape[dim] - width, None, axis=dim), axis, forward
        )
        high = lax.ppermute(lax.slice_in_dim(block, 0, width, axis=dim), axis, backward)
        block = jnp.concatenate([low, block, high], axis=dim)
    return block


def side_by_side(arrays, axis, dim, along):
    columns = [a.reshape(*a.shape[:along], -1) for a in arrays]
    both = jnp.concatenate(columns, axis=along)
    whole, at, gathered = (lax.psum_scatter(both, axis, scatter_dimension=dim, tiled=True), 0, [])
    for a, column in zip(arrays, columns):
        piece = whole[..., at : at + column.shape[along]]
        gathered.append(piece.reshape(*piece.shape[:along], *a.shape[along:]))
        at += column.shape[along]
    return tuple(gathered)


def laid_out(parts, dim):
    parts = jnp.moveaxis(parts, 0, dim)
    lengths = parts.shape
    return parts.reshape(*lengths[:dim], lengths[dim] * lengths[dim + 1], *lengths[dim + 2 :])


def from_everyone(value, axis):
    copies = jnp.broadcast_to(value, (lax.axis_size(axis), *value.shape))
    return lax.all_to_all(copies, axis, split_axis=0, concat_axis=0, tiled=True)


def gathered_copies(value, axis, dim):
    chips, cores = lax.axis_size("z"), lax.axis_size("core")
    along_z = lax.all_to_all(
        jnp.broadcast_to(value, (chips, *value.shape)), "z", split_axis=0, concat_axis=0, tiled=True
    )
    both = lax.all_to_all(
        jnp.broadcast_to(along_z, (cores, *along_z.shape)), "core", split_axis=0, concat_axis=0, tiled=True
    )
    return laid_out(jnp.swapaxes(both, 0, 1).reshape(chips * cores, *value.shape), dim)


def taper_mask(positions, live_counts):
    position = jnp.arange(BLOCK).astype(jnp.float32)
    distance = (position[None, :, None] - positions[:, None, :]) / (0.5 * BLOCK)
    active = jnp.arange(KB)[None, :] < live_counts[:, None]
    return jnp.where(active[:, None, :], 1.0 / (1.0 + distance * distance), 0.0)


def block_sums(mesh_point_entries, obs_rows):
    cross = jnp.einsum(
        "bcm,bkm->bck", mesh_point_entries, obs_rows, preferred_element_type=jnp.float32
    )
    sum_cells = jnp.sum(mesh_point_entries.astype(jnp.float32), 2)
    sum_obs = jnp.sum(obs_rows.astype(jnp.float32), 2)
    return (cross, sum_cells, sum_obs)


def covariances(cross, sum_cells, sum_obs, positions, live_counts, members):
    return (
        (cross - sum_cells[:, :, None] * sum_obs[:, None, :] / members)
        / (members - 1)
        * taper_mask(positions, live_counts)
    ).astype(jnp.bfloat16)


def apply_cov(covariance, incr_rows):
    correction_delta = jnp.einsum(
        "bck,bkm->bcm", covariance, incr_rows, preferred_element_type=jnp.float32
    )
    return correction_delta.astype(jnp.bfloat16)


def per_device(
    member_vectors,
    flow_speed_ratio,
    obs_pert,
    obs_incr,
    edge_list,
    block_obs,
    block_count,
    obs_offset,
):
    concentration_map = member_vectors
    outgoing = jnp.concatenate([concentration_map[-STEPS:, :], flow_speed_ratio[-STEPS:, None]], 1)
    arrived = passed_along(outgoing, "reg", 1)
    width = concentration_map.shape[1]
    halo = halo_rows(arrived[:, :-1], arrived[:, -1], width)
    concentration_map, first_guess_state, cell_sums = advect(halo, flow_speed_ratio, concentration_map)
    lend = edge_list.shape[2]
    edge_rows = edge_list.reshape(-1)
    own = obs_pert.shape[0]
    lent = (edge_rows[:, None] == jnp.arange(own)[None, :]).astype(jnp.bfloat16)
    member_dev = member_vectors.shape[1]
    lent_rows = jnp.dot(
        lent, jnp.concatenate([obs_pert, obs_incr], 1), preferred_element_type=jnp.float32
    ).astype(jnp.bfloat16)
    chosen = jnp.stack([lent_rows[:, :member_dev], lent_rows[:, member_dev:]])
    rimmed = padded(chosen, (("reg", 1),), lend)
    extended = jnp.concatenate(
        [rimmed[:, :lend], jnp.stack([obs_pert, obs_incr]), rimmed[:, -lend:]], 1
    )
    member_dev = member_vectors.shape[1]
    members = member_dev * lax.axis_size(MEM)
    per_region = block_obs.shape[0]
    parts = lax.axis_size(MEM)
    pairs = per_region // 2
    share = pairs // parts
    slots = extended.shape[1]
    picks = (block_obs.reshape(-1)[:, None] == jnp.arange(slots)[None, :]).astype(jnp.bfloat16)
    obs_rows = jnp.dot(picks, extended[0], preferred_element_type=jnp.float32).astype(jnp.bfloat16)
    incr_rows = jnp.dot(picks, extended[1], preferred_element_type=jnp.float32).astype(jnp.bfloat16)
    cells_p = first_guess_state.reshape(pairs, 2 * BLOCK, member_dev)
    obs_p = obs_rows.reshape(pairs, 2 * KB, member_dev)
    full = jnp.einsum("brm,blm->brl", cells_p, obs_p, preferred_element_type=jnp.float32)
    upper = (jnp.arange(2 * KB) >= KB)[None, None, :]
    cross = jnp.where(upper, full[:, BLOCK:, :], full[:, :BLOCK, :])
    sum_cells = cell_sums.reshape(pairs, 1, 2 * BLOCK)
    sum_obs = jnp.sum(obs_rows.astype(jnp.float32), 1).reshape(pairs, 1, 2 * KB)
    payload = jnp.concatenate([cross, sum_cells, sum_obs], 1)
    got = lax.psum_scatter(
        payload.reshape(parts, share, BLOCK + 2, 2 * KB), MEM, scatter_dimension=0, tiled=True
    ).reshape(share, BLOCK + 2, 2 * KB)
    cross = got[:, :BLOCK, :]
    cells_sum = jnp.transpose(got[:, BLOCK, :].reshape(share, 2, BLOCK), (0, 2, 1))
    cells_sum = jnp.broadcast_to(cells_sum[:, :, :, None], (share, BLOCK, 2, KB)).reshape(
        share, BLOCK, 2 * KB
    )
    obs_sum = got[:, BLOCK + 1, :][:, None, :]
    first_block = lax.axis_index(MEM) * share * 2
    live_counts = lax.dynamic_slice_in_dim(block_count, first_block, share * 2, 0)
    positions = lax.dynamic_slice_in_dim(obs_offset, first_block, share * 2, 0)
    position = jnp.arange(BLOCK).astype(jnp.float32)
    distance = (position[None, :, None] - positions.reshape(share, 1, 2 * KB)) / (0.5 * BLOCK)
    lane = jnp.arange(2 * KB)
    counts = live_counts.reshape(share, 2)[:, lane // KB]
    active = (lane % KB)[None, :] < counts
    taper = jnp.where(active[:, None, :], 1.0 / (1.0 + distance * distance), 0.0)
    own_cov = (
        (cross - cells_sum * obs_sum / members) / (members - 1) * taper
    ).astype(jnp.bfloat16)
    covariance = gathered_copies(own_cov, MEM, 0)
    same_block = (jnp.arange(2 * BLOCK) // BLOCK)[:, None] == (lane // KB)[None, :]
    spread = jnp.where(same_block[None], jnp.concatenate([covariance, covariance], 1), 0)
    incr_p = incr_rows.reshape(pairs, 2 * KB, member_dev)
    correction_delta = jnp.einsum(
        "brl,blm->brm", spread, incr_p, preferred_element_type=jnp.float32
    ).astype(jnp.bfloat16)
    returned = correction_delta.reshape(per_region * BLOCK, member_dev)
    return concentration_map + returned.astype(jnp.float32)


def solution(mesh):
    mem, reg = mesh.devices.shape
    split = Mesh(mesh.devices.reshape(mem // CORES, CORES, reg), ("z", "core", "reg"))
    return jax.shard_map(
        per_device,
        mesh=split,
        in_specs=(
            P("reg", MEM),
            P("reg"),
            P("reg", MEM),
            P("reg", MEM),
            P("reg", None, None),
            P("reg", None),
            P("reg"),
            P("reg", None),
        ),
        out_specs=P("reg", MEM),
        check_vma=False,
    )
```
